512 devices in a mesh: blk: 64 (over z, y_lo, core), head: 8 (over y_hi, x).
Axes of the slice: x: 4, y: 4 (y_hi: 2, y_lo: 2; y = y_hi * 2 + y_lo), z: 16, core: 2. Of those that a mesh axis runs over, the one named last changes fastest.
Arguments:
- queries: bfloat16 [12288, 4096], P(('blk', 'head'))
- key_rows: bfloat16 [12288, 1024], P(('blk', 'head'))
- value_rows: bfloat16 [12288, 1024], P(('blk', 'head')), may hold values from -6 to 6
- visit_ids: int32 [12288], replicated, may hold values from 0 to 3, as said below
- span_order: int32 [64], replicated, may hold values from 0 to 63, each once
Outputs:
- attended: bfloat16 [12288, 4096], P(('blk', 'head'))
The draws below stay inside these ranges and needn't reach their ends.
Inputs may be any that keep to these rules, and one draw needn't show every extreme that they name: `visit_ids`: visit ids never fall along time; every one of the 4 visits has events and begins at an even position. `span_order`: each block index holds a different block of 192 consecutive events.
All inputs are finite; a program needn't handle non-finite values.
Results may differ from the reference program's by a relative error of at most 0.0049.
Values may be sent and summed in bfloat16 or wider, within the bound.
No kernel may reach another device: no remote copies, remote signals or barrier semaphores. Data moves between devices by JAX's collectives and lax.ppermute only.
A program may use at most 64 MiB of HBM per device.

```python
import jax
import jax.numpy as jnp
from jax import lax

HEADS = 32
KV_HEADS = 8
HEAD_DIM = 128
BLK_ROWS = 192
VISITS = 4
LEN = 12288
SPANS = 64
KV_WIDTH = 1024


def drawn_rows(key):
    query_key = jax.random.fold_in(key, 11)
    key_key = jax.random.fold_in(key, 12)
    query_base = jnp.clip(jax.random.normal(query_key, (LEN, HEADS, HEAD_DIM), jnp.float32), -6.0, 6.0)
    key_base = jnp.clip(jax.random.normal(key_key, (LEN, KV_HEADS, HEAD_DIM), jnp.float32), -6.0, 6.0)
    return (query_base.reshape(LEN, HEADS * HEAD_DIM), key_base.reshape(LEN, KV_HEADS * HEAD_DIM))


def draw_queries(key, part):
    return drawn_rows(key)[0].astype(jnp.bfloat16)


def draw_key_rows(key, part):
    return drawn_rows(key)[1].astype(jnp.bfloat16)


def draw_visit_ids(key, part):
    pair_count = LEN // 2
    cuts = jax.random.permutation(jax.random.fold_in(key, 21), pair_count - 1)[:VISITS - 1] + 1
    pair_index = jnp.arange(pair_count, dtype=jnp.int32)
    pair_visit = jnp.sum((pair_index[:, None] >= cuts[None, :]).astype(jnp.int32), axis=1)
    return jnp.repeat(pair_visit, 2).astype(jnp.int32)


def block_levels(stream_key, shape, shards, smallest, top_value):
    factor_of, own = 1.0, jax.random.fold_in(stream_key, 6)
    for axis_at, parts in shards:
        steps = jnp.exp(jax.random.uniform(jax.random.fold_in(own, axis_at), (parts,), jnp.float32, smallest / len(shards), top_value / len(shards)))
        factor_of = factor_of * jnp.repeat(steps, shape[axis_at] // parts).reshape([-1 if axis == axis_at else 1 for axis in range(len(shape))])
    return factor_of


def gaussian(stream_key, shape, width, most, shards=(), kind=jnp.bfloat16):
    result = width * jax.random.normal(stream_key, shape, jnp.float32)
    if shards:
        result = result * block_levels(stream_key, shape, shards, -0.22, 0.18)
    return jnp.clip(result, -most, most).astype(kind)


def setup_inputs(seed: int = 0) -> dict:
    splits = jax.random.split(jax.random.key(seed), 6)
    queries = draw_queries(jax.random.fold_in(splits[5], 71), 0)
    key_rows = draw_key_rows(jax.random.fold_in(splits[5], 71), 0)
    value_rows = gaussian(splits[2], (LEN, KV_WIDTH), 1.0, 6.0, ((0, 512),))
    visit_ids = draw_visit_ids(jax.random.fold_in(splits[5], 71), 0)
    span_order = jax.random.permutation(splits[4], SPANS).astype(jnp.int32)
    return {"queries": queries, "key_rows": key_rows, "value_rows": value_rows, "visit_ids": visit_ids, "span_order": span_order}


def natural_positions(span_order):
    every_row = jnp.arange(LEN, dtype=jnp.int32)
    return (span_order[every_row // BLK_ROWS] * BLK_ROWS + every_row % BLK_ROWS).astype(jnp.int32)


def reference(queries, key_rows, value_rows, visit_ids, span_order):
    group_size = HEADS // KV_HEADS
    score_scale = HEAD_DIM ** -0.5
    positions = natural_positions(span_order)
    visits = jnp.take(visit_ids, positions)
    query_heads = queries.reshape(LEN, KV_HEADS, group_size, HEAD_DIM)
    key_heads = key_rows.reshape(LEN, KV_HEADS, HEAD_DIM)
    value_heads = value_rows.reshape(LEN, KV_HEADS, HEAD_DIM)
    block_count = LEN // BLK_ROWS

    def one_block(pair_index):
        block_index = pair_index // KV_HEADS
        head_index = pair_index % KV_HEADS
        first_row = (block_index * BLK_ROWS).astype(jnp.int32)
        query_block = lax.dynamic_slice_in_dim(query_heads, first_row, BLK_ROWS, 0)
        query_block = lax.dynamic_index_in_dim(query_block, head_index, 1, keepdims=False)
        key_head = lax.dynamic_index_in_dim(key_heads, head_index, 1, keepdims=False)
        value_head = lax.dynamic_index_in_dim(value_heads, head_index, 1, keepdims=False)
        scores = jnp.einsum("qgd,kd->qgk", query_block.astype(jnp.float32), key_head.astype(jnp.float32)) * score_scale
        query_pos = lax.dynamic_slice_in_dim(positions, first_row, BLK_ROWS, 0)
        query_visit = lax.dynamic_slice_in_dim(visits, first_row, BLK_ROWS, 0)
        allowed = (positions[None, :] <= query_pos[:, None]) & (visits[None, :] == query_visit[:, None])
        masked = jnp.where(allowed[:, None, :], scores, -jnp.inf)
        row_max = jnp.max(masked, axis=-1, keepdims=True)
        weights = jnp.where(allowed[:, None, :], jnp.exp(masked - row_max), 0.0)
        total = jnp.sum(weights, axis=-1, keepdims=True)
        rounded = lax.optimization_barrier(weights.astype(jnp.bfloat16)).astype(jnp.float32)
        mixed = jnp.einsum("qgk,kd->qgd", rounded, value_head.astype(jnp.float32)) / total
        return mixed.astype(jnp.bfloat16)

    results = lax.map(one_block, jnp.arange(block_count * KV_HEADS, dtype=jnp.int32))
    results = results.reshape(block_count, KV_HEADS, BLK_ROWS, group_size, HEAD_DIM)
    results = jnp.transpose(results, (0, 2, 1, 3, 4))
    return results.reshape(LEN, HEADS * HEAD_DIM)
```

```python
import jax
import jax.numpy as jnp
from jax import lax
from jax.experimental import pallas as pl
from jax.experimental.pallas import tpu as pltpu
from jax.sharding import Mesh, PartitionSpec as P

HEADS = 32
KV_HEADS = 8
HEAD_DIM = 128
GROUP = HEADS // KV_HEADS
SPAN_ROWS = 192
PIECE = 24
PARTS = SPAN_ROWS // PIECE
VISITS = 4
SPANS = 64
HALF = SPANS // 2
KEYS = HALF * SPAN_ROWS
PER_TILE = 4
TILE = PER_TILE * SPAN_ROWS
TILES = KEYS // TILE
SOURCES = 8
ROWS = GROUP * PIECE
SCALE_LOG2 = HEAD_DIM ** (-0.5) * 1.4426950408889634
NOTHING = -3e38

ORDER = 0
COUNT = 64
SORTED = COUNT + 65
START = SORTED + HALF
YLO = START + VISITS
CORE = YLO + 1
ZLO = YLO + 2
FIRST = YLO + 3


def gather_keys(info, own_ref, other_ref, k_buf, v_buf, sems):
    core, zlo = info[CORE], info[ZLO]
    k_pieces = k_buf.reshape(HALF * PARTS, PIECE, HEAD_DIM)
    v_pieces = v_buf.reshape(HALF * PARTS, PIECE, HEAD_DIM)

    def each(act):
        def step(i, carry):
            k, half = i // 2, i % 2
            for src, side in ((own_ref, core), (other_ref, 1 - core)):
                span = info[ORDER + (k * 2 + zlo) * 4 + half * 2 + side]
                rank = info[COUNT + span]
                for which, buf in ((0, k_pieces), (1, v_pieces)):
                    act(
                        pltpu.make_async_copy(
                            src.at[pl.ds(half * PARTS, PARTS), k, which],
                            buf.at[pl.ds(rank * PARTS, PARTS)],
                            sems.at[which, (k * 2 + half) * 2 + side],
                        )
                    )
            return carry

        lax.fori_loop(0, 2 * SOURCES, step, 0)

    each(lambda c: c.start())
    each(lambda c: c.wait())


def attend_sources(info, side, q_ref, k_buf, v_buf, s_buf, put):
    ylo, core, first = info[YLO], info[CORE], info[FIRST]
    inside = lax.rem(lax.broadcasted_iota(jnp.int32, (ROWS, HEAD_DIM), 0), PIECE)
    lane = lax.broadcasted_iota(jnp.int32, (1, HEAD_DIM), 1)

    def start_of(pos):
        low = jnp.zeros_like(pos)
        for v in range(1, VISITS):
            low = jnp.where(info[START + v] <= pos, info[START + v], low)
        return low

    def one_source(n, carry):
        span = info[ORDER + (n * 2 + side) * 4 + ylo * 2 + core]
        p0 = span * SPAN_ROWS + first
        pos = p0 + inside
        low = start_of(pos)
        low0 = start_of(p0)
        tile_a = info[COUNT + low0 // SPAN_ROWS] // PER_TILE
        tile_b = (info[COUNT + span + 1] + PER_TILE - 1) // PER_TILE
        q = q_ref[n].astype(jnp.float32).reshape(ROWS, HEAD_DIM).astype(jnp.bfloat16)

        def scores(j, best):
            base = pl.multiple_of(j * TILE, TILE)
            s = lax.dot_general(
                q,
                k_buf[pl.ds(base, TILE), :],
                (((1,), (1,)), ((), ())),
                preferred_element_type=jnp.float32,
            )
            at = [
                info[SORTED + j * PER_TILE + u] * SPAN_ROWS - u * SPAN_ROWS
                for u in range(PER_TILE)
            ]
            for c in range(TILE // HEAD_DIM):
                lo_u = c * HEAD_DIM // SPAN_ROWS
                hi_u = (c * HEAD_DIM + HEAD_DIM - 1) // SPAN_ROWS
                key = lane + c * HEAD_DIM
                if lo_u == hi_u:
                    key = key + at[lo_u]
                else:
                    key = key + jnp.where(key < hi_u * SPAN_ROWS, at[lo_u], at[hi_u])
                part = jnp.where(
                    (key >= low) & (key <= pos),
                    s[:, c * HEAD_DIM : (c + 1) * HEAD_DIM],
                    -jnp.inf,
                )
                s_buf[j, :, c * HEAD_DIM : (c + 1) * HEAD_DIM] = part
                best = jnp.maximum(best, part)
            return best

        best = lax.fori_loop(
            tile_a, tile_b, scores, jnp.full((ROWS, HEAD_DIM), -jnp.inf, jnp.float32)
        )
        top = jnp.max(best, axis=1, keepdims=True)
        some = top > -jnp.inf
        top = jnp.where(some, top, 0.0)

        def mix(j, state):
            total, acc = state
            base = pl.multiple_of(j * TILE, TILE)
            w = jnp.exp2((s_buf[j] - top) * SCALE_LOG2)
            for c in range(TILE // HEAD_DIM):
                total = total + w[:, c * HEAD_DIM : (c + 1) * HEAD_DIM]
            acc = acc + jnp.dot(
                w.astype(jnp.bfloat16),
                v_buf[pl.ds(base, TILE), :],
                preferred_element_type=jnp.float32,
            )
            return total, acc

        zero = jnp.zeros((ROWS, HEAD_DIM), jnp.float32)
        total, acc = lax.fori_loop(tile_a, tile_b, mix, (zero, zero))
        total = jnp.sum(total, axis=1, keepdims=True)
        safe = jnp.where(some, total, 1.0)
        mass = jnp.where(some, top * SCALE_LOG2 + jnp.log2(safe), NOTHING)
        put(n, (acc / safe).reshape(GROUP, PIECE, HEAD_DIM), mass)
        return carry

    lax.fori_loop(0, SOURCES, one_source, 0)


def far_kernel(info, q_ref, own_ref, other_ref, o_ref, k_buf, v_buf, s_buf, sems):
    gather_keys(info, own_ref, other_ref, k_buf, v_buf, sems)
    lane = lax.broadcasted_iota(jnp.int32, (PIECE, HEAD_DIM), 1)

    def put(n, out, mass):
        o_ref[n, :GROUP] = out.astype(jnp.bfloat16)
        packed = jnp.zeros((PIECE, HEAD_DIM), jnp.float32)
        high = mass.astype(jnp.bfloat16).astype(jnp.float32)
        rest = mass - high
        middle = rest.astype(jnp.bfloat16).astype(jnp.float32)
        pieces = (high, middle, rest - middle)
        for g in range(GROUP):
            for i, piece in enumerate(pieces):
                packed = jnp.where(
                    lane == 3 * g + i, piece[g * PIECE : (g + 1) * PIECE], packed
                )
        o_ref[n, GROUP] = packed.astype(jnp.bfloat16)

    attend_sources(info, 1 - info[ZLO], q_ref, k_buf, v_buf, s_buf, put)


def near_kernel(info, q_ref, k_buf, v_buf, o_ref, m_ref, s_buf):
    def put(n, out, mass):
        o_ref[n] = out
        m_ref[n] = jnp.broadcast_to(mass, (ROWS, HEAD_DIM)).reshape(
            GROUP, PIECE, HEAD_DIM
        )

    attend_sources(info, info[ZLO], q_ref, k_buf, v_buf, s_buf, put)


def merge_kernel(near_ref, mass_ref, far_ref, o_ref):
    for n in range(SOURCES):
        packed = far_ref[n, GROUP].astype(jnp.float32)
        for g in range(GROUP):
            a = mass_ref[n, g]
            b = (
                packed[:, 3 * g : 3 * g + 1]
                + packed[:, 3 * g + 1 : 3 * g + 2]
                + packed[:, 3 * g + 2 : 3 * g + 3]
            )
            m = jnp.maximum(a, b)
            wa, wb = jnp.exp2(a - m), jnp.exp2(b - m)
            out = (wa * near_ref[n, g] + wb * far_ref[n, g].astype(jnp.float32)) / (wa + wb)
            o_ref[n, :, g * HEAD_DIM : (g + 1) * HEAD_DIM] = out.astype(jnp.bfloat16)


def pack_kernel(q_ref, k_ref, v_ref, o_ref):
    for h in range(KV_HEADS):
        o_ref[h, 0] = k_ref[:, h * HEAD_DIM : (h + 1) * HEAD_DIM]
        o_ref[h, 1] = v_ref[:, h * HEAD_DIM : (h + 1) * HEAD_DIM]
        for g in range(GROUP):
            c = (h * GROUP + g) * HEAD_DIM
            o_ref[h, 2 + g] = q_ref[:, c : c + HEAD_DIM]


SMEM = pl.BlockSpec(memory_space=pltpu.SMEM)
VMEM = pl.BlockSpec(memory_space=pltpu.VMEM)
ANY = pl.BlockSpec(memory_space=pl.ANY)
COST = pl.CostEstimate(flops=6_000_000_000, bytes_accessed=4_000_000, transcendentals=4_000_000)


def shape(*sizes, kind=jnp.bfloat16):
    return jax.ShapeDtypeStruct(sizes, kind)


SCORES = pltpu.VMEM((TILES, ROWS, TILE), jnp.float32)
SMALL = pltpu.CompilerParams(vmem_limit_bytes=8 << 20)
LIMIT = pltpu.CompilerParams(vmem_limit_bytes=32 << 20)


def far_part(info, q, own, other):
    return pl.pallas_call(
        far_kernel,
        out_shape=(
            shape(SOURCES, GROUP + 1, PIECE, HEAD_DIM),
            shape(KEYS, HEAD_DIM),
            shape(KEYS, HEAD_DIM),
        ),
        in_specs=[SMEM, VMEM, ANY, ANY],
        out_specs=(VMEM, VMEM, VMEM),
        scratch_shapes=[SCORES, pltpu.SemaphoreType.DMA((2, HALF))],
        compiler_params=LIMIT,
        cost_estimate=COST,
        name="far",
    )(info, q, own, other)


def near_part(info, q, k, v):
    return pl.pallas_call(
        near_kernel,
        out_shape=(
            shape(SOURCES, GROUP, PIECE, HEAD_DIM, kind=jnp.float32),
            shape(SOURCES, GROUP, PIECE, HEAD_DIM, kind=jnp.float32),
        ),
        in_specs=[SMEM, VMEM, VMEM, VMEM],
        out_specs=(VMEM, VMEM),
        scratch_shapes=[SCORES],
        compiler_params=LIMIT,
        cost_estimate=COST,
        name="near",
    )(info, q, k, v)


def merge(near, mass, far):
    return pl.pallas_call(
        merge_kernel,
        out_shape=shape(SOURCES, PIECE, GROUP * HEAD_DIM),
        in_specs=[VMEM, VMEM, VMEM],
        out_specs=VMEM,
        compiler_params=SMALL,
        name="merge",
    )(near, mass, far)


def pack(q, k, v):
    return pl.pallas_call(
        pack_kernel,
        out_shape=shape(KV_HEADS, GROUP + 2, PIECE, HEAD_DIM),
        in_specs=[VMEM, VMEM, VMEM],
        out_specs=VMEM,
        compiler_params=SMALL,
        name="pack",
    )(q, k, v)


PLANE = ("ylo", "yhi", "x")
SWAP = [(0, 1), (1, 0)]


def table(visit_ids, span_order):
    zlo = lax.axis_index("zlo").astype(jnp.int32)
    block = jnp.arange(SPANS, dtype=jnp.int32)
    mine = (block // 4) % 2 == zlo
    upto = jnp.arange(SPANS + 1, dtype=jnp.int32)
    count = jnp.sum(
        (mine[None, :] & (span_order[None, :] < upto[:, None])).astype(jnp.int32), axis=1
    )
    ranks = jnp.arange(HALF, dtype=jnp.int32)
    ordered = jnp.sum((count[None, 1:] <= ranks[:, None]).astype(jnp.int32), axis=1)
    starts = jnp.sum(
        (visit_ids[None, :] < jnp.arange(VISITS, dtype=jnp.int32)[:, None]).astype(jnp.int32),
        axis=1,
    )
    place = jnp.stack(
        [
            lax.axis_index("ylo"),
            lax.axis_index("core"),
            lax.axis_index("zlo"),
            (lax.axis_index("yhi") * 4 + lax.axis_index("x")) * PIECE,
        ]
    ).astype(jnp.int32)
    return jnp.concatenate([span_order, count, ordered, starts, place])


def body(queries, key_rows, value_rows, visit_ids, span_order):
    info = table(visit_ids, span_order)
    packed = lax.all_to_all(pack(queries, key_rows, value_rows), "zhi", 0, 0, tiled=True)
    near_q = packed[:, 2:]
    far_q = lax.ppermute(near_q, "zlo", SWAP)
    kv = packed[:, :2]
    spread = jnp.broadcast_to(kv[None], (16,) + kv.shape)
    own = lax.all_to_all(spread, PLANE, 0, 0, tiled=True)
    other = lax.ppermute(own, "core", SWAP)

    far_out, k, v = far_part(info, far_q, own, other)
    sent = lax.ppermute(far_out, "zlo", SWAP)
    near_out, mass = near_part(info, near_q, k, v)
    out = merge(near_out, mass, sent)
    out = lax.all_to_all(out, "zhi", 0, 0, tiled=True)
    return jnp.transpose(out, (1, 0, 2)).reshape(PIECE, HEADS * HEAD_DIM)


def solution(mesh):
    fine = Mesh(
        mesh.devices.reshape(8, 2, 2, 2, 2, 4), ("zhi", "zlo", "ylo", "core", "yhi", "x")
    )
    rows = P(("zhi", "zlo", "ylo", "core", "yhi", "x"), None)
    return jax.shard_map(
        body,
        mesh=fine,
        in_specs=(rows, rows, rows, P(), P()),
        out_specs=rows,
        check_vma=False,
    )
```

```python
import jax
import jax.numpy as jnp
from jax import lax
from jax.experimental import pallas as pl
from jax.experimental.pallas import tpu as pltpu
from jax.sharding import Mesh, PartitionSpec as P

HEADS = 32
KV_HEADS = 8
HEAD_DIM = 128
GROUP = HEADS // KV_HEADS
SPAN_ROWS = 192
PIECE = 24
PARTS = SPAN_ROWS // PIECE
VISITS = 4
SPANS = 64
HALF = SPANS // 2
KEYS = HALF * SPAN_ROWS
PER_TILE = 4
UNROLL = 2
TILE = PER_TILE * SPAN_ROWS
TILES = KEYS // TILE
SOURCES = 8
ROWS = GROUP * PIECE
SCALE_LOG2 = HEAD_DIM ** (-0.5) * 1.4426950408889634
NOTHING = -3e38

ORDER = 0
COUNT = 64
SORTED = COUNT + 65
START = SORTED + HALF
YLO = START + VISITS
CORE = YLO + 1
ZLO = YLO + 2
FIRST = YLO + 3


def gather_keys(info, own_ref, other_ref, buf, which, sems):
    core, zlo = info[CORE], info[ZLO]
    pieces = buf.reshape(HALF * PARTS, PIECE, HEAD_DIM)

    def each(act):
        def step(i, carry):
            k, half = i // 2, i % 2
            for src, side in ((own_ref, core), (other_ref, 1 - core)):
                span = info[ORDER + (k * 2 + zlo) * 4 + half * 2 + side]
                rank = info[COUNT + span]
                act(
                    pltpu.make_async_copy(
                        src.at[pl.ds(half * PARTS, PARTS), k, which],
                        pieces.at[pl.ds(rank * PARTS, PARTS)],
                        sems.at[which, (k * 2 + half) * 2 + side],
                    )
                )
            return carry

        lax.fori_loop(0, 2 * SOURCES, step, 0)

    return lambda: each(lambda c: c.start()), lambda: each(lambda c: c.wait())


def attend_sources(info, side, q_ref, k_buf, v_buf, scratch, put, k_ready, v_ready):
    s_buf, q_buf, low_buf, pos_buf, best, top_buf, total, acc, item_n, item_j = scratch
    ylo, core, first = info[YLO], info[CORE], info[FIRST]
    inside = lax.broadcasted_iota(jnp.int32, (PIECE, HEAD_DIM), 0)
    lane = lax.broadcasted_iota(jnp.int32, (1, HEAD_DIM), 1)

    def start_of(pos):
        low = jnp.zeros_like(pos)
        for v in range(1, VISITS):
            low = jnp.where(info[START + v] <= pos, info[START + v], low)
        return low

    count = jnp.int32(0)
    for n in range(SOURCES):
        span = info[ORDER + (n * 2 + side) * 4 + ylo * 2 + core]
        p0 = span * SPAN_ROWS + first
        pos = p0 + inside
        pos_buf[n] = pos
        low_buf[n] = start_of(pos)
        q_buf[n] = (
            q_ref[n, 2:].astype(jnp.float32).reshape(ROWS, HEAD_DIM).astype(jnp.bfloat16)
        )
        tile_a = info[COUNT + start_of(p0) // SPAN_ROWS] // PER_TILE
        tile_b = (info[COUNT + span + 1] + PER_TILE - 1) // PER_TILE

        def note(j, at, n=n):
            item_n[at] = n
            item_j[at] = j
            return at + 1

        count = lax.fori_loop(tile_a, tile_b, note, count)
    for u in range(UNROLL - 1):
        item_n[count + u] = SOURCES
        item_j[count + u] = 0
    steps = (count + UNROLL - 1) // UNROLL

    for n in range(SOURCES):
        for u in range(UNROLL):
            best[u, n] = jnp.full((ROWS, HEAD_DIM), -jnp.inf, jnp.float32)
            total[u, n] = jnp.zeros((ROWS, HEAD_DIM), jnp.float32)
            acc[u, n] = jnp.zeros((ROWS, HEAD_DIM), jnp.float32)

    k_ready()

    def scores(i, carry):
        for u in range(UNROLL):
            at = i * UNROLL + u
            slot, j = item_n[at], item_j[at]
            n = jnp.minimum(slot, SOURCES - 1)
            s = lax.dot_general(
                q_buf[n],
                k_buf[pl.ds(pl.multiple_of(j * TILE, TILE), TILE), :],
                (((1,), (1,)), ((), ())),
                preferred_element_type=jnp.float32,
            )
            s = s.reshape(GROUP, PIECE, TILE)
            low, pos = low_buf[n], pos_buf[n]
            base = [
                (info[SORTED + j * PER_TILE + w] - w) * SPAN_ROWS for w in range(PER_TILE)
            ]
            high = best[u, slot].reshape(GROUP, PIECE, HEAD_DIM)
            for c in range(TILE // HEAD_DIM):
                left = c * HEAD_DIM // SPAN_ROWS
                right = (c * HEAD_DIM + HEAD_DIM - 1) // SPAN_ROWS
                key = lane + c * HEAD_DIM
                if left == right:
                    key = key + base[left]
                else:
                    key = key + jnp.where(key < right * SPAN_ROWS, base[left], base[right])
                keep = (key >= low) & (key <= pos)
                part = jnp.where(
                    keep[None], s[:, :, c * HEAD_DIM : (c + 1) * HEAD_DIM], -jnp.inf
                )
                s_buf[at, :, c * HEAD_DIM : (c + 1) * HEAD_DIM] = part.reshape(ROWS, HEAD_DIM)
                high = jnp.maximum(high, part)
            best[u, slot] = high.reshape(ROWS, HEAD_DIM)
        return carry

    lax.fori_loop(0, steps, scores, 0)

    for n in range(SOURCES):
        high = best[0, n]
        for u in range(1, UNROLL):
            high = jnp.maximum(high, best[u, n])
        top = jnp.max(high, axis=1, keepdims=True)
        top_buf[n] = jnp.broadcast_to(top, (ROWS, HEAD_DIM))

    v_ready()

    def mix(i, carry):
        for u in range(UNROLL):
            at = i * UNROLL + u
            slot, j = item_n[at], item_j[at]
            n = jnp.minimum(slot, SOURCES - 1)
            top = top_buf[n]
            top = jnp.where(top > -jnp.inf, top, 0.0)
            part_sum = total[u, slot]
            parts = []
            for c in range(TILE // HEAD_DIM):
                w = jnp.exp2(
                    (s_buf[at, :, c * HEAD_DIM : (c + 1) * HEAD_DIM] - top) * SCALE_LOG2
                )
                part_sum = part_sum + w
                parts.append(w.astype(jnp.bfloat16))
            total[u, slot] = part_sum
            acc[u, slot] = acc[u, slot] + jnp.dot(
                jnp.concatenate(parts, axis=1),
                v_buf[pl.ds(pl.multiple_of(j * TILE, TILE), TILE), :],
                preferred_element_type=jnp.float32,
            )
        return carry

    lax.fori_loop(0, steps, mix, 0)

    for n in range(SOURCES):
        top = top_buf[n]
        whole, out = total[0, n], acc[0, n]
        for u in range(1, UNROLL):
            whole, out = whole + total[u, n], out + acc[u, n]
        whole = jnp.sum(whole, axis=1, keepdims=True)
        some = top > -jnp.inf
        safe = jnp.where(some, whole, 1.0)
        mass = jnp.where(some, top * SCALE_LOG2 + jnp.log2(safe), NOTHING)
        put(
            n,
            (out / safe).reshape(GROUP, PIECE, HEAD_DIM),
            mass.reshape(GROUP, PIECE, HEAD_DIM),
        )


def far_kernel(info, q_ref, own_ref, other_ref, o_ref, k_buf, v_buf, sems, *scratch):
    k_start, k_ready = gather_keys(info, own_ref, other_ref, k_buf, 0, sems)
    v_start, v_ready = gather_keys(info, own_ref, other_ref, v_buf, 1, sems)
    k_start()
    v_start()
    lane = lax.broadcasted_iota(jnp.int32, (PIECE, HEAD_DIM), 1)

    def put(n, out, mass):
        o_ref[n, :GROUP] = out.astype(jnp.bfloat16)
        high = mass.astype(jnp.bfloat16).astype(jnp.float32)
        rest = mass - high
        middle = rest.astype(jnp.bfloat16).astype(jnp.float32)
        pieces = (high, middle, rest - middle)
        packed = jnp.zeros((PIECE, HEAD_DIM), jnp.float32)
        for g in range(GROUP):
            for i, piece in enumerate(pieces):
                packed = jnp.where(lane == 3 * g + i, piece[g], packed)
        o_ref[n, GROUP] = packed.astype(jnp.bfloat16)

    attend_sources(
        info, 1 - info[ZLO], q_ref, k_buf, v_buf, scratch, put, k_ready, v_ready
    )


def near_kernel(info, q_ref, k_buf, v_buf, o_ref, m_ref, *scratch):
    def put(n, out, mass):
        o_ref[n] = out
        m_ref[n] = mass

    nothing = lambda: None
    attend_sources(info, info[ZLO], q_ref, k_buf, v_buf, scratch, put, nothing, nothing)


def merge_kernel(near_ref, mass_ref, far_ref, o_ref):
    for n in range(SOURCES):
        packed = far_ref[n, GROUP].astype(jnp.float32)
        for g in range(GROUP):
            a = mass_ref[n, g]
            b = (
                packed[:, 3 * g : 3 * g + 1]
                + packed[:, 3 * g + 1 : 3 * g + 2]
                + packed[:, 3 * g + 2 : 3 * g + 3]
            )
            m = jnp.maximum(a, b)
            wa, wb = jnp.exp2(a - m), jnp.exp2(b - m)
            out = (wa * near_ref[n, g] + wb * far_ref[n, g].astype(jnp.float32)) / (wa + wb)
            o_ref[n, :, g * HEAD_DIM : (g + 1) * HEAD_DIM] = out.astype(jnp.bfloat16)


def pack_kernel(q_ref, k_ref, v_ref, o_ref, sems):
    copies = []
    for h in range(KV_HEADS):
        for i in range(GROUP + 2):
            src, c = ((k_ref, h), (v_ref, h))[i] if i < 2 else (q_ref, h * GROUP + i - 2)
            copies.append(
                pltpu.make_async_copy(
                    src.at[:, c * HEAD_DIM : (c + 1) * HEAD_DIM], o_ref.at[h, i], sems.at[h, i]
                )
            )
    for c in copies:
        c.start()
    for c in copies:
        c.wait()


def fan_kernel(packed_ref, o_ref):
    for i in range(16):
        o_ref[i] = packed_ref[:, :2]


SMEM = pl.BlockSpec(memory_space=pltpu.SMEM)
VMEM = pl.BlockSpec(memory_space=pltpu.VMEM)
ANY = pl.BlockSpec(memory_space=pl.ANY)
HBM = pl.BlockSpec(memory_space=pltpu.HBM)
COST = pl.CostEstimate(flops=6_000_000_000, bytes_accessed=4_000_000, transcendentals=4_000_000)


def shape(*sizes, kind=jnp.bfloat16):
    return jax.ShapeDtypeStruct(sizes, kind)


ITEMS = SOURCES * TILES + UNROLL
SCRATCH = [
    pltpu.VMEM((ITEMS, ROWS, TILE), jnp.float32),
    pltpu.VMEM((SOURCES, ROWS, HEAD_DIM), jnp.bfloat16),
    pltpu.VMEM((SOURCES, PIECE, HEAD_DIM), jnp.int32),
    pltpu.VMEM((SOURCES, PIECE, HEAD_DIM), jnp.int32),
    pltpu.VMEM((UNROLL, SOURCES + 1, ROWS, HEAD_DIM), jnp.float32),
    pltpu.VMEM((SOURCES, ROWS, HEAD_DIM), jnp.float32),
    pltpu.VMEM((UNROLL, SOURCES + 1, ROWS, HEAD_DIM), jnp.float32),
    pltpu.VMEM((UNROLL, SOURCES + 1, ROWS, HEAD_DIM), jnp.float32),
    pltpu.SMEM((ITEMS,), jnp.int32),
    pltpu.SMEM((ITEMS,), jnp.int32),
]
SMALL = pltpu.CompilerParams(vmem_limit_bytes=8 << 20)
LIMIT = pltpu.CompilerParams(vmem_limit_bytes=40 << 20)


def far_part(info, q, own, other):
    return pl.pallas_call(
        far_kernel,
        out_shape=(
            shape(SOURCES, GROUP + 1, PIECE, HEAD_DIM),
            shape(KEYS, HEAD_DIM),
            shape(KEYS, HEAD_DIM),
        ),
        in_specs=[SMEM, VMEM, ANY, ANY],
        out_specs=(VMEM, VMEM, VMEM),
        scratch_shapes=[pltpu.SemaphoreType.DMA((2, HALF))] + SCRATCH,
        compiler_params=LIMIT,
        cost_estimate=COST,
        name="far",
    )(info, q, own, other)


def near_part(info, q, k, v):
    return pl.pallas_call(
        near_kernel,
        out_shape=(
            shape(SOURCES, GROUP, PIECE, HEAD_DIM, kind=jnp.float32),
            shape(SOURCES, GROUP, PIECE, HEAD_DIM, kind=jnp.float32),
        ),
        in_specs=[SMEM, VMEM, VMEM, VMEM],
        out_specs=(VMEM, VMEM),
        scratch_shapes=SCRATCH,
        compiler_params=LIMIT,
        cost_estimate=COST,
        name="near",
    )(info, q, k, v)


def merge(near, mass, far):
    return pl.pallas_call(
        merge_kernel,
        out_shape=shape(SOURCES, PIECE, GROUP * HEAD_DIM),
        in_specs=[VMEM, VMEM, VMEM],
        out_specs=VMEM,
        compiler_params=SMALL,
        name="merge",
    )(near, mass, far)


def pack(q, k, v):
    return pl.pallas_call(
        pack_kernel,
        out_shape=shape(KV_HEADS, GROUP + 2, PIECE, HEAD_DIM),
        in_specs=[HBM, HBM, HBM],
        out_specs=VMEM,
        scratch_shapes=[pltpu.SemaphoreType.DMA((KV_HEADS, GROUP + 2))],
        name="pack",
    )(q, k, v)


def fan(packed):
    return pl.pallas_call(
        fan_kernel,
        out_shape=shape(16, SOURCES, 2, PIECE, HEAD_DIM),
        in_specs=[VMEM],
        out_specs=VMEM,
        compiler_params=SMALL,
        name="fan",
    )(packed)


PLANE = ("ylo", "yhi", "x")
SWAP = [(0, 1), (1, 0)]


def table(visit_ids, span_order):
    zlo = lax.axis_index("zlo").astype(jnp.int32)
    block = jnp.arange(SPANS, dtype=jnp.int32)
    mine = (block // 4) % 2 == zlo
    upto = jnp.arange(SPANS + 1, dtype=jnp.int32)
    count = jnp.sum(
        (mine[None, :] & (span_order[None, :] < upto[:, None])).astype(jnp.int32), axis=1
    )
    ranks = jnp.arange(HALF, dtype=jnp.int32)
    ordered = jnp.sum((count[None, 1:] <= ranks[:, None]).astype(jnp.int32), axis=1)
    starts = jnp.sum(
        (visit_ids[None, :] < jnp.arange(VISITS, dtype=jnp.int32)[:, None]).astype(jnp.int32),
        axis=1,
    )
    place = jnp.stack(
        [
            lax.axis_index("ylo"),
            lax.axis_index("core"),
            lax.axis_index("zlo"),
            (lax.axis_index("yhi") * 4 + lax.axis_index("x")) * PIECE,
        ]
    ).astype(jnp.int32)
    return jnp.concatenate([span_order, count, ordered, starts, place])


def body(queries, key_rows, value_rows, visit_ids, span_order):
    info = table(visit_ids, span_order)
    packed = lax.all_to_all(pack(queries, key_rows, value_rows), "zhi", 0, 0, tiled=True)
    far_q = lax.ppermute(packed, "zlo", SWAP)
    spread = fan(packed)
    own = lax.all_to_all(spread, PLANE, 0, 0, tiled=True)
    other = lax.ppermute(own, "core", SWAP)

    far_out, k, v = far_part(info, far_q, own, other)
    sent = lax.ppermute(far_out, "zlo", SWAP)
    near_out, mass = near_part(info, packed, k, v)
    out = merge(near_out, mass, sent)
    out = lax.all_to_all(out, "zhi", 0, 0, tiled=True)
    return jnp.transpose(out, (1, 0, 2)).reshape(PIECE, HEADS * HEAD_DIM)


def solution(mesh):
    fine = Mesh(
        mesh.devices.reshape(8, 2, 2, 2, 2, 4), ("zhi", "zlo", "ylo", "core", "yhi", "x")
    )
    rows = P(("zhi", "zlo", "ylo", "core", "yhi", "x"), None)
    return jax.shard_map(
        body,
        mesh=fine,
        in_specs=(rows, rows, rows, P(), P()),
        out_specs=rows,
        check_vma=False,
    )
```

```python
import jax
import jax.numpy as jnp
from jax import lax
from jax.experimental import pallas as pl
from jax.experimental.pallas import tpu as pltpu
from jax.sharding import Mesh, PartitionSpec as P

HEADS = 32
KV_HEADS = 8
HEAD_DIM = 128
GROUP = HEADS // KV_HEADS
SPAN_ROWS = 192
PIECE = 24
PARTS = SPAN_ROWS // PIECE
VISITS = 4
SPANS = 64
HALF = SPANS // 2
KEYS = HALF * SPAN_ROWS
PER_TILE = 4
UNROLL = 4
TILE = PER_TILE * SPAN_ROWS
TILES = KEYS // TILE
SOURCES = 8
ROWS = GROUP * PIECE
SCALE_LOG2 = HEAD_DIM ** (-0.5) * 1.4426950408889634
NOTHING = -3e38

ORDER = 0
COUNT = 64
SORTED = COUNT + 65
START = SORTED + HALF
YLO = START + VISITS
CORE = YLO + 1
ZLO = YLO + 2
FIRST = YLO + 3


def key_copies(info, src, side, buf, which, sems):
    zlo = info[ZLO]
    pieces = buf.reshape(HALF * PARTS, PIECE, HEAD_DIM)

    def each(act, by_y):
        def step(i, carry):
            k, half = i // 2, i % 2
            span = info[ORDER + (k * 2 + zlo) * 4 + half * 2 + side]
            rank = info[COUNT + span]
            for yhi in range(2):
                y = half * 2 + yhi
                rows = src.at[y, :, k, which] if by_y else src.at[:, y, k, which]
                act(
                    pltpu.make_async_copy(
                        rows,
                        pieces.at[pl.ds(rank * PARTS + yhi * 4, 4)],
                        sems.at[which, i, yhi],
                    )
                )
            return carry

        lax.fori_loop(0, 2 * SOURCES, step, 0)

    def start():
        for by_y in (True, False):
            pl.when(side == (0 if by_y else 1))(
                lambda by_y=by_y: each(lambda c: c.start(), by_y)
            )

    return start, lambda: each(lambda c: c.wait(), True)


def attend_sources(info, side, q_ref, k_buf, v_buf, scratch, put, k_ready, v_ready):
    s_buf, q_buf, low_buf, pos_buf, best, top_buf, total, acc, item_n, item_j = scratch
    ylo, core, first = info[YLO], info[CORE], info[FIRST]
    inside = lax.broadcasted_iota(jnp.int32, (PIECE, HEAD_DIM), 0)
    lane = lax.broadcasted_iota(jnp.int32, (1, HEAD_DIM), 1)

    def start_of(pos):
        low = jnp.zeros_like(pos)
        for v in range(1, VISITS):
            low = jnp.where(info[START + v] <= pos, info[START + v], low)
        return low

    count = jnp.int32(0)
    for n in range(SOURCES):
        span = info[ORDER + (n * 2 + side) * 4 + ylo * 2 + core]
        p0 = span * SPAN_ROWS + first
        pos = p0 + inside
        pos_buf[n] = pos
        low_buf[n] = start_of(pos)
        q_buf[n] = (
            q_ref[n, 2:].astype(jnp.float32).reshape(ROWS, HEAD_DIM).astype(jnp.bfloat16)
        )
        tile_a = info[COUNT + start_of(p0) // SPAN_ROWS] // PER_TILE
        tile_b = (info[COUNT + span + 1] + PER_TILE - 1) // PER_TILE

        def note(j, at, n=n):
            item_n[at] = n
            item_j[at] = j
            return at + 1

        count = lax.fori_loop(tile_a, tile_b, note, count)
    for u in range(UNROLL - 1):
        item_n[count + u] = SOURCES
        item_j[count + u] = 0
    steps = (count + UNROLL - 1) // UNROLL

    for n in range(SOURCES):
        for u in range(UNROLL):
            best[u, n] = jnp.full((ROWS, HEAD_DIM), -jnp.inf, jnp.float32)
            total[u, n] = jnp.zeros((ROWS, HEAD_DIM), jnp.float32)
            acc[u, n] = jnp.zeros((ROWS, HEAD_DIM), jnp.float32)

    k_ready()

    def scores(i, carry):
        for u in range(UNROLL):
            at = i * UNROLL + u
            slot, j = item_n[at], item_j[at]
            n = jnp.minimum(slot, SOURCES - 1)
            s = lax.dot_general(
                q_buf[n],
                k_buf[pl.ds(pl.multiple_of(j * TILE, TILE), TILE), :],
                (((1,), (1,)), ((), ())),
                preferred_element_type=jnp.float32,
            )
            s = s.reshape(GROUP, PIECE, TILE)
            low, pos = low_buf[n], pos_buf[n]
            base = [
                (info[SORTED + j * PER_TILE + w] - w) * SPAN_ROWS for w in range(PER_TILE)
            ]
            high = best[u, slot].reshape(GROUP, PIECE, HEAD_DIM)
            for c in range(TILE // HEAD_DIM):
                left = c * HEAD_DIM // SPAN_ROWS
                right = (c * HEAD_DIM + HEAD_DIM - 1) // SPAN_ROWS
                key = lane + c * HEAD_DIM
                if left == right:
                    key = key + base[left]
                else:
                    key = key + jnp.where(key < right * SPAN_ROWS, base[left], base[right])
                keep = (key >= low) & (key <= pos)
                part = jnp.where(
                    keep[None], s[:, :, c * HEAD_DIM : (c + 1) * HEAD_DIM], -jnp.inf
                )
                s_buf[at, :, c * HEAD_DIM : (c + 1) * HEAD_DIM] = part.reshape(ROWS, HEAD_DIM)
                high = jnp.maximum(high, part)
            best[u, slot] = high.reshape(ROWS, HEAD_DIM)
        return carry

    lax.fori_loop(0, steps, scores, 0)

    for n in range(SOURCES):
        high = best[0, n]
        for u in range(1, UNROLL):
            high = jnp.maximum(high, best[u, n])
        top = jnp.max(high, axis=1, keepdims=True)
        top_buf[n] = jnp.broadcast_to(top, (ROWS, HEAD_DIM))

    v_ready()

    def mix(i, carry):
        for u in range(UNROLL):
            at = i * UNROLL + u
            slot, j = item_n[at], item_j[at]
            n = jnp.minimum(slot, SOURCES - 1)
            top = top_buf[n]
            top = jnp.where(top > -jnp.inf, top, 0.0)
            part_sum = total[u, slot]
            parts = []
            for c in range(TILE // HEAD_DIM):
                w = jnp.exp2(
                    (s_buf[at, :, c * HEAD_DIM : (c + 1) * HEAD_DIM] - top) * SCALE_LOG2
                )
                part_sum = part_sum + w
                parts.append(w.astype(jnp.bfloat16))
            total[u, slot] = part_sum
            acc[u, slot] = acc[u, slot] + jnp.dot(
                jnp.concatenate(parts, axis=1),
                v_buf[pl.ds(pl.multiple_of(j * TILE, TILE), TILE), :],
                preferred_element_type=jnp.float32,
            )
        return carry

    lax.fori_loop(0, steps, mix, 0)

    for n in range(SOURCES):
        top = top_buf[n]
        whole, out = total[0, n], acc[0, n]
        for u in range(1, UNROLL):
            whole, out = whole + total[u, n], out + acc[u, n]
        whole = jnp.sum(whole, axis=1, keepdims=True)
        some = top > -jnp.inf
        safe = jnp.where(some, whole, 1.0)
        mass = jnp.where(some, top * SCALE_LOG2 + jnp.log2(safe), NOTHING)
        put(
            n,
            (out / safe).reshape(GROUP, PIECE, HEAD_DIM),
            mass.reshape(GROUP, PIECE, HEAD_DIM),
        )


def order_kernel(info, own_ref, k_buf, v_buf, sems):
    parts = [
        key_copies(info, own_ref, info[CORE], buf, which, sems)
        for which, buf in ((0, k_buf), (1, v_buf))
    ]
    for start, _ in parts:
        start()
    for _, ready in parts:
        ready()


def far_kernel(
    info, q_ref, other_ref, k_half, v_half, o_ref, k_buf, v_buf, sems, *scratch
):
    side = 1 - info[CORE]
    k_start, k_ready = key_copies(info, other_ref, side, k_buf, 0, sems)
    v_start, v_ready = key_copies(info, other_ref, side, v_buf, 1, sems)
    k_start()
    v_start()
    lane = lax.broadcasted_iota(jnp.int32, (PIECE, HEAD_DIM), 1)

    def put(n, out, mass):
        o_ref[n, :GROUP] = out.astype(jnp.bfloat16)
        high = mass.astype(jnp.bfloat16).astype(jnp.float32)
        rest = mass - high
        middle = rest.astype(jnp.bfloat16).astype(jnp.float32)
        pieces = (high, middle, rest - middle)
        packed = jnp.zeros((PIECE, HEAD_DIM), jnp.float32)
        for g in range(GROUP):
            for i, piece in enumerate(pieces):
                packed = jnp.where(lane == 3 * g + i, piece[g], packed)
        o_ref[n, GROUP] = packed.astype(jnp.bfloat16)

    attend_sources(
        info, 1 - info[ZLO], q_ref, k_buf, v_buf, scratch, put, k_ready, v_ready
    )


def near_kernel(info, q_ref, k_buf, v_buf, o_ref, m_ref, *scratch):
    def put(n, out, mass):
        o_ref[n] = out
        m_ref[n] = mass

    nothing = lambda: None
    attend_sources(info, info[ZLO], q_ref, k_buf, v_buf, scratch, put, nothing, nothing)


def merge_kernel(near_ref, mass_ref, far_ref, o_ref):
    for n in range(SOURCES):
        packed = far_ref[n, GROUP].astype(jnp.float32)
        for g in range(GROUP):
            a = mass_ref[n, g]
            b = (
                packed[:, 3 * g : 3 * g + 1]
                + packed[:, 3 * g + 1 : 3 * g + 2]
                + packed[:, 3 * g + 2 : 3 * g + 3]
            )
            m = jnp.maximum(a, b)
            wa, wb = jnp.exp2(a - m), jnp.exp2(b - m)
            out = (wa * near_ref[n, g] + wb * far_ref[n, g].astype(jnp.float32)) / (wa + wb)
            o_ref[n, :, g * HEAD_DIM : (g + 1) * HEAD_DIM] = out.astype(jnp.bfloat16)


def pack_kernel(q_ref, k_ref, v_ref, o_ref, sems):
    copies = []
    for h in range(KV_HEADS):
        for i in range(GROUP + 2):
            src, c = ((k_ref, h), (v_ref, h))[i] if i < 2 else (q_ref, h * GROUP + i - 2)
            copies.append(
                pltpu.make_async_copy(
                    src.at[:, c * HEAD_DIM : (c + 1) * HEAD_DIM], o_ref.at[h, i], sems.at[h, i]
                )
            )
    for c in copies:
        c.start()
    for c in copies:
        c.wait()


def fan_first_kernel(packed_ref, o_ref):
    for i in range(4):
        o_ref[i] = packed_ref[:, :2]


def fan_second_kernel(line_ref, o_ref):
    for i in range(4):
        o_ref[i] = line_ref[...]


SMEM = pl.BlockSpec(memory_space=pltpu.SMEM)
VMEM = pl.BlockSpec(memory_space=pltpu.VMEM)
ANY = pl.BlockSpec(memory_space=pl.ANY)
HBM = pl.BlockSpec(memory_space=pltpu.HBM)
COST = pl.CostEstimate(flops=6_000_000_000, bytes_accessed=4_000_000, transcendentals=4_000_000)


def shape(*sizes, kind=jnp.bfloat16):
    return jax.ShapeDtypeStruct(sizes, kind)


ITEMS = SOURCES * TILES + UNROLL
SCRATCH = [
    pltpu.VMEM((ITEMS, ROWS, TILE), jnp.float32),
    pltpu.VMEM((SOURCES, ROWS, HEAD_DIM), jnp.bfloat16),
    pltpu.VMEM((SOURCES, PIECE, HEAD_DIM), jnp.int32),
    pltpu.VMEM((SOURCES, PIECE, HEAD_DIM), jnp.int32),
    pltpu.VMEM((UNROLL, SOURCES + 1, ROWS, HEAD_DIM), jnp.float32),
    pltpu.VMEM((SOURCES, ROWS, HEAD_DIM), jnp.float32),
    pltpu.VMEM((UNROLL, SOURCES + 1, ROWS, HEAD_DIM), jnp.float32),
    pltpu.VMEM((UNROLL, SOURCES + 1, ROWS, HEAD_DIM), jnp.float32),
    pltpu.SMEM((ITEMS,), jnp.int32),
    pltpu.SMEM((ITEMS,), jnp.int32),
]
SMALL = pltpu.CompilerParams(vmem_limit_bytes=8 << 20)
LIMIT = pltpu.CompilerParams(vmem_limit_bytes=40 << 20)


SEMS = pltpu.SemaphoreType.DMA((2, 2 * SOURCES, 2))


def order_part(info, own):
    return pl.pallas_call(
        order_kernel,
        out_shape=(shape(KEYS, HEAD_DIM), shape(KEYS, HEAD_DIM)),
        in_specs=[SMEM, ANY],
        out_specs=(VMEM, VMEM),
        scratch_shapes=[SEMS],
        compiler_params=SMALL,
        cost_estimate=pl.CostEstimate(flops=0, bytes_accessed=6_000_000, transcendentals=0),
        name="order",
    )(info, own)


def far_part(info, q, other, k, v):
    return pl.pallas_call(
        far_kernel,
        out_shape=(
            shape(SOURCES, GROUP + 1, PIECE, HEAD_DIM),
            shape(KEYS, HEAD_DIM),
            shape(KEYS, HEAD_DIM),
        ),
        in_specs=[SMEM, VMEM, ANY, VMEM, VMEM],
        out_specs=(VMEM, VMEM, VMEM),
        scratch_shapes=[SEMS] + SCRATCH,
        input_output_aliases={3: 1, 4: 2},
        compiler_params=LIMIT,
        cost_estimate=COST,
        name="far",
    )(info, q, other, k, v)


def near_part(info, q, k, v):
    return pl.pallas_call(
        near_kernel,
        out_shape=(
            shape(SOURCES, GROUP, PIECE, HEAD_DIM, kind=jnp.float32),
            shape(SOURCES, GROUP, PIECE, HEAD_DIM, kind=jnp.float32),
        ),
        in_specs=[SMEM, VMEM, VMEM, VMEM],
        out_specs=(VMEM, VMEM),
        scratch_shapes=SCRATCH,
        compiler_params=LIMIT,
        cost_estimate=COST,
        name="near",
    )(info, q, k, v)


def merge(near, mass, far):
    return pl.pallas_call(
        merge_kernel,
        out_shape=shape(SOURCES, PIECE, GROUP * HEAD_DIM),
        in_specs=[VMEM, VMEM, VMEM],
        out_specs=VMEM,
        compiler_params=SMALL,
        name="merge",
    )(near, mass, far)


def pack(q, k, v):
    return pl.pallas_call(
        pack_kernel,
        out_shape=shape(KV_HEADS, GROUP + 2, PIECE, HEAD_DIM),
        in_specs=[HBM, HBM, HBM],
        out_specs=VMEM,
        scratch_shapes=[pltpu.SemaphoreType.DMA((KV_HEADS, GROUP + 2))],
        name="pack",
    )(q, k, v)


def fan(kernel, source, *sizes):
    return pl.pallas_call(
        kernel,
        out_shape=shape(*sizes, SOURCES, 2, PIECE, HEAD_DIM),
        in_specs=[VMEM],
        out_specs=VMEM,
        compiler_params=SMALL,
        name="fan",
    )(source)


SWAP = [(0, 1), (1, 0)]


def place_of(ylo, core, yhi, x):
    return ((ylo * 2 + core) * 2 + yhi) * 4 + x


def lines(core, along_x):
    ys = [(ylo, yhi) for ylo in range(2) for yhi in range(2)]
    if along_x:
        return [[place_of(ylo, core, yhi, x) for x in range(4)] for ylo, yhi in ys]
    return [[place_of(ylo, core, yhi, x) for ylo, yhi in ys] for x in range(4)]


def spread(rows, along_x):
    return lax.all_to_all(
        rows,
        "plane",
        0,
        0,
        axis_index_groups=lines(0, along_x) + lines(1, not along_x),
        tiled=True,
    )


def table(visit_ids, span_order):
    zlo = lax.axis_index("zlo").astype(jnp.int32)
    block = jnp.arange(SPANS, dtype=jnp.int32)
    mine = (block // 4) % 2 == zlo
    upto = jnp.arange(SPANS + 1, dtype=jnp.int32)
    count = jnp.sum(
        (mine[None, :] & (span_order[None, :] < upto[:, None])).astype(jnp.int32), axis=1
    )
    ranks = jnp.arange(HALF, dtype=jnp.int32)
    ordered = jnp.sum((count[None, 1:] <= ranks[:, None]).astype(jnp.int32), axis=1)
    starts = jnp.sum(
        (visit_ids[None, :] < jnp.arange(VISITS, dtype=jnp.int32)[:, None]).astype(jnp.int32),
        axis=1,
    )
    at = lax.axis_index("plane")
    place = jnp.stack([at // 16, at // 8 % 2, zlo, at % 8 * PIECE]).astype(jnp.int32)
    return jnp.concatenate([span_order, count, ordered, starts, place])


def body(queries, key_rows, value_rows, visit_ids, span_order):
    info = table(visit_ids, span_order)
    packed = pack(queries, key_rows, value_rows)
    packed = lax.all_to_all(packed, "zhi", 0, 0, tiled=True)
    far_q = lax.ppermute(packed, "zlo", SWAP)
    line = fan(fan_first_kernel, packed, 4)
    line = spread(line, True)
    own = fan(fan_second_kernel, line, 4, 4)
    own = spread(own, False)
    other = lax.ppermute(own, "plane", [(i, i ^ 8) for i in range(32)])
    k, v = order_part(info, own)

    far_out, k, v = far_part(info, far_q, other, k, v)
    sent = lax.ppermute(far_out, "zlo", SWAP)
    near_out, mass = near_part(info, packed, k, v)
    out = merge(near_out, mass, sent)
    out = lax.all_to_all(out, "zhi", 0, 0, tiled=True)
    return jnp.transpose(out, (1, 0, 2)).reshape(PIECE, HEADS * HEAD_DIM)


def solution(mesh):
    fine = Mesh(mesh.devices.reshape(8, 2, 32), ("zhi", "zlo", "plane"))
    rows = P(("zhi", "zlo", "plane"), None)
    return jax.shard_map(
        body,
        mesh=fine,
        in_specs=(rows, rows, rows, P(), P()),
        out_specs=rows,
        check_vma=False,
    )
```

```python
import jax
import jax.numpy as jnp
from jax import lax
from jax.experimental import pallas as pl
from jax.experimental.pallas import tpu as pltpu
from jax.sharding import Mesh, PartitionSpec as P

HEADS = 32
KV_HEADS = 8
HEAD_DIM = 128
GROUP = HEADS // KV_HEADS
SPAN_ROWS = 192
PIECE = 24
PARTS = SPAN_ROWS // PIECE
VISITS = 4
SPANS = 64
HALF = SPANS // 2
KEYS = HALF * SPAN_ROWS
PER_TILE = 4
UNROLL = 4
TILE = PER_TILE * SPAN_ROWS
TILES = KEYS // TILE
SOURCES = 8
ROWS = GROUP * PIECE
SCALE_LOG2 = HEAD_DIM ** (-0.5) * 1.4426950408889634
NOTHING = -3e38

ORDER = 0
COUNT = 64
SORTED = COUNT + 65
START = SORTED + HALF
YLO = START + VISITS
CORE = YLO + 1
ZLO = YLO + 2
FIRST = YLO + 3


def key_copies(info, src, side, buf, which, sems):
    zlo = info[ZLO]
    pieces = buf.reshape(HALF * PARTS, PIECE, HEAD_DIM)

    def each(act):
        def step(i, carry):
            k, half = i // 2, i % 2
            span = info[ORDER + (k * 2 + zlo) * 4 + half * 2 + side]
            rank = info[COUNT + span]
            act(
                pltpu.make_async_copy(
                    src.at[pl.ds(half * PARTS, PARTS), k, which],
                    pieces.at[pl.ds(rank * PARTS, PARTS)],
                    sems.at[which, i],
                )
            )
            return carry

        lax.fori_loop(0, 2 * SOURCES, step, 0)

    return lambda: each(lambda c: c.start()), lambda: each(lambda c: c.wait())


def attend_sources(info, side, q_ref, k_buf, v_buf, scratch, put, k_ready, v_ready):
    s_buf, q_buf, low_buf, pos_buf, best, top_buf, total, acc, item_n, item_j = scratch
    ylo, core, first = info[YLO], info[CORE], info[FIRST]
    inside = lax.broadcasted_iota(jnp.int32, (PIECE, HEAD_DIM), 0)
    lane = lax.broadcasted_iota(jnp.int32, (1, HEAD_DIM), 1)

    def start_of(pos):
        low = jnp.zeros_like(pos)
        for v in range(1, VISITS):
            low = jnp.where(info[START + v] <= pos, info[START + v], low)
        return low

    count = jnp.int32(0)
    for n in range(SOURCES):
        span = info[ORDER + (n * 2 + side) * 4 + ylo * 2 + core]
        p0 = span * SPAN_ROWS + first
        pos = p0 + inside
        pos_buf[n] = pos
        low_buf[n] = start_of(pos)
        q_buf[n] = (
            q_ref[n, 2:].astype(jnp.float32).reshape(ROWS, HEAD_DIM).astype(jnp.bfloat16)
        )
        tile_a = info[COUNT + start_of(p0) // SPAN_ROWS] // PER_TILE
        tile_b = (info[COUNT + span + 1] + PER_TILE - 1) // PER_TILE

        def note(j, at, n=n):
            item_n[at] = n
            item_j[at] = j
            return at + 1

        count = lax.fori_loop(tile_a, tile_b, note, count)
    for u in range(UNROLL - 1):
        item_n[count + u] = SOURCES
        item_j[count + u] = 0
    steps = (count + UNROLL - 1) // UNROLL

    for n in range(SOURCES):
        for u in range(UNROLL):
            best[u, n] = jnp.full((ROWS, HEAD_DIM), -jnp.inf, jnp.float32)
            total[u, n] = jnp.zeros((ROWS, HEAD_DIM), jnp.float32)
            acc[u, n] = jnp.zeros((ROWS, HEAD_DIM), jnp.float32)

    k_ready()

    def scores(i, carry):
        for u in range(UNROLL):
            at = i * UNROLL + u
            slot, j = item_n[at], item_j[at]
            n = jnp.minimum(slot, SOURCES - 1)
            s = lax.dot_general(
                q_buf[n],
                k_buf[pl.ds(pl.multiple_of(j * TILE, TILE), TILE), :],
                (((1,), (1,)), ((), ())),
                preferred_element_type=jnp.float32,
            )
            s = s.reshape(GROUP, PIECE, TILE)
            low, pos = low_buf[n], pos_buf[n]
            base = [
                (info[SORTED + j * PER_TILE + w] - w) * SPAN_ROWS for w in range(PER_TILE)
            ]
            high = best[u, slot].reshape(GROUP, PIECE, HEAD_DIM)
            for c in range(TILE // HEAD_DIM):
                left = c * HEAD_DIM // SPAN_ROWS
                right = (c * HEAD_DIM + HEAD_DIM - 1) // SPAN_ROWS
                key = lane + c * HEAD_DIM
                if left == right:
                    key = key + base[left]
                else:
                    key = key + jnp.where(key < right * SPAN_ROWS, base[left], base[right])
                keep = (key >= low) & (key <= pos)
                part = jnp.where(
                    keep[None], s[:, :, c * HEAD_DIM : (c + 1) * HEAD_DIM], -jnp.inf
                )
                s_buf[at, :, c * HEAD_DIM : (c + 1) * HEAD_DIM] = part.reshape(ROWS, HEAD_DIM)
                high = jnp.maximum(high, part)
            best[u, slot] = high.reshape(ROWS, HEAD_DIM)
        return carry

    lax.fori_loop(0, steps, scores, 0)

    for n in range(SOURCES):
        high = best[0, n]
        for u in range(1, UNROLL):
            high = jnp.maximum(high, best[u, n])
        top = jnp.max(high, axis=1, keepdims=True)
        top_buf[n] = jnp.broadcast_to(top, (ROWS, HEAD_DIM))

    v_ready()

    def mix(i, carry):
        for u in range(UNROLL):
            at = i * UNROLL + u
            slot, j = item_n[at], item_j[at]
            n = jnp.minimum(slot, SOURCES - 1)
            top = top_buf[n]
            top = jnp.where(top > -jnp.inf, top, 0.0)
            part_sum = total[u, slot]
            parts = []
            for c in range(TILE // HEAD_DIM):
                w = jnp.exp2(
                    (s_buf[at, :, c * HEAD_DIM : (c + 1) * HEAD_DIM] - top) * SCALE_LOG2
                )
                part_sum = part_sum + w
                parts.append(w.astype(jnp.bfloat16))
            total[u, slot] = part_sum
            acc[u, slot] = acc[u, slot] + jnp.dot(
                jnp.concatenate(parts, axis=1),
                v_buf[pl.ds(pl.multiple_of(j * TILE, TILE), TILE), :],
                preferred_element_type=jnp.float32,
            )
        return carry

    lax.fori_loop(0, steps, mix, 0)

    for n in range(SOURCES):
        top = top_buf[n]
        whole, out = total[0, n], acc[0, n]
        for u in range(1, UNROLL):
            whole, out = whole + total[u, n], out + acc[u, n]
        whole = jnp.sum(whole, axis=1, keepdims=True)
        some = top > -jnp.inf
        safe = jnp.where(some, whole, 1.0)
        mass = jnp.where(some, top * SCALE_LOG2 + jnp.log2(safe), NOTHING)
        put(
            n,
            (out / safe).reshape(GROUP, PIECE, HEAD_DIM),
            mass.reshape(GROUP, PIECE, HEAD_DIM),
        )


def order_kernel(info, own_ref, k_buf, v_buf, sems):
    parts = [
        key_copies(info, own_ref, info[CORE], buf, which, sems)
        for which, buf in ((0, k_buf), (1, v_buf))
    ]
    for start, _ in parts:
        start()
    for _, ready in parts:
        ready()


def far_kernel(
    info, q_ref, other_ref, k_half, v_half, o_ref, k_buf, v_buf, sems, *scratch
):
    side = 1 - info[CORE]
    k_start, k_ready = key_copies(info, other_ref, side, k_buf, 0, sems)
    v_start, v_ready = key_copies(info, other_ref, side, v_buf, 1, sems)
    k_start()
    v_start()
    lane = lax.broadcasted_iota(jnp.int32, (PIECE, HEAD_DIM), 1)

    def put(n, out, mass):
        o_ref[n, :GROUP] = out.astype(jnp.bfloat16)
        high = mass.astype(jnp.bfloat16).astype(jnp.float32)
        rest = mass - high
        middle = rest.astype(jnp.bfloat16).astype(jnp.float32)
        pieces = (high, middle, rest - middle)
        packed = jnp.zeros((PIECE, HEAD_DIM), jnp.float32)
        for g in range(GROUP):
            for i, piece in enumerate(pieces):
                packed = jnp.where(lane == 3 * g + i, piece[g], packed)
        o_ref[n, GROUP] = packed.astype(jnp.bfloat16)

    attend_sources(
        info, 1 - info[ZLO], q_ref, k_buf, v_buf, scratch, put, k_ready, v_ready
    )


def near_kernel(info, q_ref, k_buf, v_buf, o_ref, m_ref, *scratch):
    def put(n, out, mass):
        o_ref[n] = out
        m_ref[n] = mass

    nothing = lambda: None
    attend_sources(info, info[ZLO], q_ref, k_buf, v_buf, scratch, put, nothing, nothing)


def merge_kernel(near_ref, mass_ref, far_ref, o_ref):
    for n in range(SOURCES):
        packed = far_ref[n, GROUP].astype(jnp.float32)
        for g in range(GROUP):
            a = mass_ref[n, g]
            b = (
                packed[:, 3 * g : 3 * g + 1]
                + packed[:, 3 * g + 1 : 3 * g + 2]
                + packed[:, 3 * g + 2 : 3 * g + 3]
            )
            m = jnp.maximum(a, b)
            wa, wb = jnp.exp2(a - m), jnp.exp2(b - m)
            out = (wa * near_ref[n, g] + wb * far_ref[n, g].astype(jnp.float32)) / (wa + wb)
            o_ref[n, :, g * HEAD_DIM : (g + 1) * HEAD_DIM] = out.astype(jnp.bfloat16)


def pack_kernel(q_ref, k_ref, v_ref, o_ref, sems):
    copies = []
    for h in range(KV_HEADS):
        for i in range(GROUP + 2):
            src, c = ((k_ref, h), (v_ref, h))[i] if i < 2 else (q_ref, h * GROUP + i - 2)
            copies.append(
                pltpu.make_async_copy(
                    src.at[:, c * HEAD_DIM : (c + 1) * HEAD_DIM], o_ref.at[h, i], sems.at[h, i]
                )
            )
    for c in copies:
        c.start()
    for c in copies:
        c.wait()


def fan_kernel(packed_ref, o_ref):
    for i in range(16):
        o_ref[i] = packed_ref[:, :2]


SMEM = pl.BlockSpec(memory_space=pltpu.SMEM)
VMEM = pl.BlockSpec(memory_space=pltpu.VMEM)
ANY = pl.BlockSpec(memory_space=pl.ANY)
HBM = pl.BlockSpec(memory_space=pltpu.HBM)
COST = pl.CostEstimate(flops=6_000_000_000, bytes_accessed=4_000_000, transcendentals=4_000_000)


def shape(*sizes, kind=jnp.bfloat16):
    return jax.ShapeDtypeStruct(sizes, kind)


ITEMS = SOURCES * TILES + UNROLL
SCRATCH = [
    pltpu.VMEM((ITEMS, ROWS, TILE), jnp.float32),
    pltpu.VMEM((SOURCES, ROWS, HEAD_DIM), jnp.bfloat16),
    pltpu.VMEM((SOURCES, PIECE, HEAD_DIM), jnp.int32),
    pltpu.VMEM((SOURCES, PIECE, HEAD_DIM), jnp.int32),
    pltpu.VMEM((UNROLL, SOURCES + 1, ROWS, HEAD_DIM), jnp.float32),
    pltpu.VMEM((SOURCES, ROWS, HEAD_DIM), jnp.float32),
    pltpu.VMEM((UNROLL, SOURCES + 1, ROWS, HEAD_DIM), jnp.float32),
    pltpu.VMEM((UNROLL, SOURCES + 1, ROWS, HEAD_DIM), jnp.float32),
    pltpu.SMEM((ITEMS,), jnp.int32),
    pltpu.SMEM((ITEMS,), jnp.int32),
]
SMALL = pltpu.CompilerParams(vmem_limit_bytes=8 << 20)
LIMIT = pltpu.CompilerParams(vmem_limit_bytes=40 << 20)


SEMS = pltpu.SemaphoreType.DMA((2, 2 * SOURCES))


def order_part(info, own):
    return pl.pallas_call(
        order_kernel,
        out_shape=(shape(KEYS, HEAD_DIM), shape(KEYS, HEAD_DIM)),
        in_specs=[SMEM, ANY],
        out_specs=(VMEM, VMEM),
        scratch_shapes=[SEMS],
        compiler_params=SMALL,
        cost_estimate=pl.CostEstimate(flops=0, bytes_accessed=6_000_000, transcendentals=0),
        name="order",
    )(info, own)


def far_part(info, q, other, k, v):
    return pl.pallas_call(
        far_kernel,
        out_shape=(
            shape(SOURCES, GROUP + 1, PIECE, HEAD_DIM),
            shape(KEYS, HEAD_DIM),
            shape(KEYS, HEAD_DIM),
        ),
        in_specs=[SMEM, VMEM, ANY, VMEM, VMEM],
        out_specs=(VMEM, VMEM, VMEM),
        scratch_shapes=[SEMS] + SCRATCH,
        input_output_aliases={3: 1, 4: 2},
        compiler_params=LIMIT,
        cost_estimate=COST,
        name="far",
    )(info, q, other, k, v)


def near_part(info, q, k, v):
    return pl.pallas_call(
        near_kernel,
        out_shape=(
            shape(SOURCES, GROUP, PIECE, HEAD_DIM, kind=jnp.float32),
            shape(SOURCES, GROUP, PIECE, HEAD_DIM, kind=jnp.float32),
        ),
        in_specs=[SMEM, VMEM, VMEM, VMEM],
        out_specs=(VMEM, VMEM),
        scratch_shapes=SCRATCH,
        compiler_params=LIMIT,
        cost_estimate=COST,
        name="near",
    )(info, q, k, v)


def merge(near, mass, far):
    return pl.pallas_call(
        merge_kernel,
        out_shape=shape(SOURCES, PIECE, GROUP * HEAD_DIM),
        in_specs=[VMEM, VMEM, VMEM],
        out_specs=VMEM,
        compiler_params=SMALL,
        name="merge",
    )(near, mass, far)


def pack(q, k, v):
    return pl.pallas_call(
        pack_kernel,
        out_shape=shape(KV_HEADS, GROUP + 2, PIECE, HEAD_DIM),
        in_specs=[HBM, HBM, HBM],
        out_specs=VMEM,
        scratch_shapes=[pltpu.SemaphoreType.DMA((KV_HEADS, GROUP + 2))],
        name="pack",
    )(q, k, v)


def fan(packed):
    return pl.pallas_call(
        fan_kernel,
        out_shape=shape(16, SOURCES, 2, PIECE, HEAD_DIM),
        in_specs=[VMEM],
        out_specs=VMEM,
        compiler_params=SMALL,
        name="fan",
    )(packed)


SWAP = [(0, 1), (1, 0)]
PLANE = [
    [((ylo * 2 + core) * 2 + yhi) * 4 + x for ylo in range(2) for yhi in range(2) for x in range(4)]
    for core in range(2)
]


def table(visit_ids, span_order):
    zlo = lax.axis_index("zlo").astype(jnp.int32)
    block = jnp.arange(SPANS, dtype=jnp.int32)
    mine = (block // 4) % 2 == zlo
    upto = jnp.arange(SPANS + 1, dtype=jnp.int32)
    count = jnp.sum(
        (mine[None, :] & (span_order[None, :] < upto[:, None])).astype(jnp.int32), axis=1
    )
    ranks = jnp.arange(HALF, dtype=jnp.int32)
    ordered = jnp.sum((count[None, 1:] <= ranks[:, None]).astype(jnp.int32), axis=1)
    starts = jnp.sum(
        (visit_ids[None, :] < jnp.arange(VISITS, dtype=jnp.int32)[:, None]).astype(jnp.int32),
        axis=1,
    )
    at = lax.axis_index("plane")
    place = jnp.stack([at // 16, at // 8 % 2, zlo, at % 8 * PIECE]).astype(jnp.int32)
    return jnp.concatenate([span_order, count, ordered, starts, place])


def body(queries, key_rows, value_rows, visit_ids, span_order):
    info = table(visit_ids, span_order)
    packed = pack(queries, key_rows, value_rows)
    packed = lax.all_to_all(packed, "zhi", 0, 0, tiled=True)
    far_q = lax.ppermute(packed, "zlo", SWAP)
    spread = fan(packed)
    own = lax.all_to_all(
        spread, "plane", 0, 0, axis_index_groups=PLANE, tiled=True
    )
    other = lax.ppermute(own, "plane", [(i, i ^ 8) for i in range(32)])
    k, v = order_part(info, own)

    far_out, k, v = far_part(info, far_q, other, k, v)
    sent = lax.ppermute(far_out, "zlo", SWAP)
    near_out, mass = near_part(info, packed, k, v)
    out = merge(near_out, mass, sent)
    out = lax.all_to_all(out, "zhi", 0, 0, tiled=True)
    return jnp.transpose(out, (1, 0, 2)).reshape(PIECE, HEADS * HEAD_DIM)


def solution(mesh):
    fine = Mesh(mesh.devices.reshape(8, 2, 32), ("zhi", "zlo", "plane"))
    rows = P(("zhi", "zlo", "plane"), None)
    return jax.shard_map(
        body,
        mesh=fine,
        in_specs=(rows, rows, rows, P(), P()),
        out_specs=rows,
        check_vma=False,
    )
```

```python
import jax
import jax.numpy as jnp
from jax import lax
from jax.experimental import pallas as pl
from jax.experimental.pallas import tpu as pltpu
from jax.sharding import Mesh, PartitionSpec as P

HEADS = 32
KV_HEADS = 8
HEAD_DIM = 128
GROUP = HEADS // KV_HEADS
SPAN_ROWS = 192
PIECE = 24
PARTS = SPAN_ROWS // PIECE
VISITS = 4
SPANS = 64
HALF = SPANS // 2
KEYS = HALF * SPAN_ROWS
PER_TILE = 4
UNROLL = 4
TILE = PER_TILE * SPAN_ROWS
TILES = KEYS // TILE
SOURCES = 8
ROWS = GROUP * PIECE
SCALE_LOG2 = HEAD_DIM ** (-0.5) * 1.4426950408889634
NOTHING = -3e38

ORDER = 0
COUNT = 64
SORTED = COUNT + 65
START = SORTED + HALF
YLO = START + VISITS
CORE = YLO + 1
ZLO = YLO + 2
FIRST = YLO + 3
TOTAL = YLO + 4
LIST = TOTAL + 2
ITEMS = SOURCES * TILES + UNROLL


def take_keys(info, src, side, k_buf, v_buf):
    zlo = info[ZLO]
    pieces = [buf.reshape(HALF * PARTS, PIECE, HEAD_DIM) for buf in (k_buf, v_buf)]

    def step(i, carry):
        k, half = i // 2, i % 2
        span = info[ORDER + (k * 2 + zlo) * 4 + half * 2 + side]
        rank = info[COUNT + span]
        for part in range(PARTS):
            for which, buf in enumerate(pieces):
                buf[rank * PARTS + part] = src[half * PARTS + part, k, which]
        return carry

    lax.fori_loop(0, 2 * SOURCES, step, 0)


def attend_sources(info, side, q_ref, k_buf, v_buf, scratch, put):
    s_buf, q_buf, low_buf, pos_buf, best, top_buf, total, acc = scratch
    ylo, core, first = info[YLO], info[CORE], info[FIRST]
    inside = lax.broadcasted_iota(jnp.int32, (PIECE, HEAD_DIM), 0)
    lane = lax.broadcasted_iota(jnp.int32, (1, HEAD_DIM), 1)

    def start_of(pos):
        low = jnp.zeros_like(pos)
        for v in range(1, VISITS):
            low = jnp.where(info[START + v] <= pos, info[START + v], low)
        return low

    for n in range(SOURCES):
        span = info[ORDER + (n * 2 + side) * 4 + ylo * 2 + core]
        pos = span * SPAN_ROWS + first + inside
        pos_buf[n] = pos
        low_buf[n] = start_of(pos)
        q_buf[n] = (
            q_ref[n, 2:].astype(jnp.float32).reshape(ROWS, HEAD_DIM).astype(jnp.bfloat16)
        )
        best[n] = jnp.full((ROWS, HEAD_DIM), -jnp.inf, jnp.float32)
        total[n] = jnp.zeros((ROWS, HEAD_DIM), jnp.float32)
        acc[n] = jnp.zeros((ROWS, HEAD_DIM), jnp.float32)
    far = jnp.where(side == info[ZLO], 0, 1)
    steps = (info[TOTAL + far] + UNROLL - 1) // UNROLL
    listed = LIST + far * ITEMS

    def item(at):
        entry = info[listed + at]
        return entry // 16, entry % 16

    def scores(i, carry):
        for u in range(UNROLL):
            at = i * UNROLL + u
            slot, j = item(at)
            n = jnp.minimum(slot, SOURCES - 1)
            s = lax.dot_general(
                q_buf[n],
                k_buf[pl.ds(pl.multiple_of(j * TILE, TILE), TILE), :],
                (((1,), (1,)), ((), ())),
                preferred_element_type=jnp.float32,
            )
            s = s.reshape(GROUP, PIECE, TILE)
            low, pos = low_buf[n], pos_buf[n]
            base = [
                (info[SORTED + j * PER_TILE + w] - w) * SPAN_ROWS for w in range(PER_TILE)
            ]
            high = best[slot].reshape(GROUP, PIECE, HEAD_DIM)
            for c in range(TILE // HEAD_DIM):
                left = c * HEAD_DIM // SPAN_ROWS
                right = (c * HEAD_DIM + HEAD_DIM - 1) // SPAN_ROWS
                key = lane + c * HEAD_DIM
                if left == right:
                    key = key + base[left]
                else:
                    key = key + jnp.where(key < right * SPAN_ROWS, base[left], base[right])
                keep = (key >= low) & (key <= pos)
                part = jnp.where(
                    keep[None], s[:, :, c * HEAD_DIM : (c + 1) * HEAD_DIM], -jnp.inf
                )
                s_buf[at, :, c * HEAD_DIM : (c + 1) * HEAD_DIM] = part.reshape(ROWS, HEAD_DIM)
                high = jnp.maximum(high, part)
            best[slot] = high.reshape(ROWS, HEAD_DIM)
        return carry

    lax.fori_loop(0, steps, scores, 0)

    for n in range(SOURCES):
        top = jnp.max(best[n], axis=1, keepdims=True)
        top_buf[n] = jnp.broadcast_to(top, (ROWS, HEAD_DIM))

    def mix(i, carry):
        for u in range(UNROLL):
            at = i * UNROLL + u
            slot, j = item(at)
            n = jnp.minimum(slot, SOURCES - 1)
            top = top_buf[n]
            top = jnp.where(top > -jnp.inf, top, 0.0)
            part_sum = total[slot]
            parts = []
            for c in range(TILE // HEAD_DIM):
                w = jnp.exp2(
                    (s_buf[at, :, c * HEAD_DIM : (c + 1) * HEAD_DIM] - top) * SCALE_LOG2
                )
                part_sum = part_sum + w
                parts.append(w.astype(jnp.bfloat16))
            total[slot] = part_sum
            acc[slot] = acc[slot] + jnp.dot(
                jnp.concatenate(parts, axis=1),
                v_buf[pl.ds(pl.multiple_of(j * TILE, TILE), TILE), :],
                preferred_element_type=jnp.float32,
            )
        return carry

    lax.fori_loop(0, steps, mix, 0)

    for n in range(SOURCES):
        top = top_buf[n]
        whole, out = jnp.sum(total[n], axis=1, keepdims=True), acc[n]
        some = top > -jnp.inf
        safe = jnp.where(some, whole, 1.0)
        mass = jnp.where(some, top * SCALE_LOG2 + jnp.log2(safe), NOTHING)
        put(
            n,
            (out / safe).reshape(GROUP, PIECE, HEAD_DIM),
            mass.reshape(GROUP, PIECE, HEAD_DIM),
        )


def order_kernel(info, own_ref, k_buf, v_buf):
    take_keys(info, own_ref, info[CORE], k_buf, v_buf)


def far_kernel(info, q_ref, other_ref, k_half, v_half, o_ref, k_buf, v_buf, *scratch):
    take_keys(info, other_ref, 1 - info[CORE], k_buf, v_buf)
    lane = lax.broadcasted_iota(jnp.int32, (PIECE, HEAD_DIM), 1)

    def put(n, out, mass):
        o_ref[n, :GROUP] = out.astype(jnp.bfloat16)
        high = mass.astype(jnp.bfloat16).astype(jnp.float32)
        rest = mass - high
        middle = rest.astype(jnp.bfloat16).astype(jnp.float32)
        pieces = (high, middle, rest - middle)
        packed = jnp.zeros((PIECE, HEAD_DIM), jnp.float32)
        for g in range(GROUP):
            for i, piece in enumerate(pieces):
                packed = jnp.where(lane == 3 * g + i, piece[g], packed)
        o_ref[n, GROUP] = packed.astype(jnp.bfloat16)

    attend_sources(info, 1 - info[ZLO], q_ref, k_buf, v_buf, scratch, put)


def near_kernel(info, q_ref, k_buf, v_buf, o_ref, m_ref, *scratch):
    def put(n, out, mass):
        o_ref[n] = out
        m_ref[n] = mass

    attend_sources(info, info[ZLO], q_ref, k_buf, v_buf, scratch, put)


def merge_kernel(near_ref, mass_ref, far_ref, o_ref):
    for n in range(SOURCES):
        packed = far_ref[n, GROUP].astype(jnp.float32)
        for g in range(GROUP):
            a = mass_ref[n, g]
            b = (
                packed[:, 3 * g : 3 * g + 1]
                + packed[:, 3 * g + 1 : 3 * g + 2]
                + packed[:, 3 * g + 2 : 3 * g + 3]
            )
            m = jnp.maximum(a, b)
            wa, wb = jnp.exp2(a - m), jnp.exp2(b - m)
            out = (wa * near_ref[n, g] + wb * far_ref[n, g].astype(jnp.float32)) / (wa + wb)
            o_ref[n, :, g * HEAD_DIM : (g + 1) * HEAD_DIM] = out.astype(jnp.bfloat16)


def pack_kernel(q_ref, k_ref, v_ref, o_ref, sems):
    copies = []
    for h in range(KV_HEADS):
        for i in range(GROUP + 2):
            src, c = ((k_ref, h), (v_ref, h))[i] if i < 2 else (q_ref, h * GROUP + i - 2)
            copies.append(
                pltpu.make_async_copy(
                    src.at[:, c * HEAD_DIM : (c + 1) * HEAD_DIM], o_ref.at[h, i], sems.at[h, i]
                )
            )
    for c in copies:
        c.start()
    for c in copies:
        c.wait()


def fan_kernel(packed_ref, o_ref):
    for i in range(16):
        o_ref[i] = packed_ref[:, :2]


SMEM = pl.BlockSpec(memory_space=pltpu.SMEM)
VMEM = pl.BlockSpec(memory_space=pltpu.VMEM)
HBM = pl.BlockSpec(memory_space=pltpu.HBM)
COST = pl.CostEstimate(flops=6_000_000_000, bytes_accessed=4_000_000, transcendentals=4_000_000)


def shape(*sizes, kind=jnp.bfloat16):
    return jax.ShapeDtypeStruct(sizes, kind)


SCRATCH = [
    pltpu.VMEM((ITEMS, ROWS, TILE), jnp.float32),
    pltpu.VMEM((SOURCES, ROWS, HEAD_DIM), jnp.bfloat16),
    pltpu.VMEM((SOURCES, PIECE, HEAD_DIM), jnp.int32),
    pltpu.VMEM((SOURCES, PIECE, HEAD_DIM), jnp.int32),
    pltpu.VMEM((SOURCES + 1, ROWS, HEAD_DIM), jnp.float32),
    pltpu.VMEM((SOURCES, ROWS, HEAD_DIM), jnp.float32),
    pltpu.VMEM((SOURCES + 1, ROWS, HEAD_DIM), jnp.float32),
    pltpu.VMEM((SOURCES + 1, ROWS, HEAD_DIM), jnp.float32),
]
SMALL = pltpu.CompilerParams(vmem_limit_bytes=8 << 20)
LIMIT = pltpu.CompilerParams(vmem_limit_bytes=40 << 20)


def order_part(info, own):
    return pl.pallas_call(
        order_kernel,
        out_shape=(shape(KEYS, HEAD_DIM), shape(KEYS, HEAD_DIM)),
        in_specs=[SMEM, VMEM],
        out_specs=(VMEM, VMEM),
        compiler_params=SMALL,
        cost_estimate=pl.CostEstimate(flops=0, bytes_accessed=6_000_000, transcendentals=0),
        name="order",
    )(info, own)


def far_part(info, q, other, k, v):
    return pl.pallas_call(
        far_kernel,
        out_shape=(
            shape(SOURCES, GROUP + 1, PIECE, HEAD_DIM),
            shape(KEYS, HEAD_DIM),
            shape(KEYS, HEAD_DIM),
        ),
        in_specs=[SMEM, VMEM, VMEM, VMEM, VMEM],
        out_specs=(VMEM, VMEM, VMEM),
        scratch_shapes=SCRATCH,
        input_output_aliases={3: 1, 4: 2},
        compiler_params=LIMIT,
        cost_estimate=COST,
        name="far",
    )(info, q, other, k, v)


def near_part(info, q, k, v):
    return pl.pallas_call(
        near_kernel,
        out_shape=(
            shape(SOURCES, GROUP, PIECE, HEAD_DIM, kind=jnp.float32),
            shape(SOURCES, GROUP, PIECE, HEAD_DIM, kind=jnp.float32),
        ),
        in_specs=[SMEM, VMEM, VMEM, VMEM],
        out_specs=(VMEM, VMEM),
        scratch_shapes=SCRATCH,
        compiler_params=LIMIT,
        cost_estimate=COST,
        name="near",
    )(info, q, k, v)


def merge(near, mass, far):
    return pl.pallas_call(
        merge_kernel,
        out_shape=shape(SOURCES, PIECE, GROUP * HEAD_DIM),
        in_specs=[VMEM, VMEM, VMEM],
        out_specs=VMEM,
        compiler_params=SMALL,
        name="merge",
    )(near, mass, far)


def pack(q, k, v):
    return pl.pallas_call(
        pack_kernel,
        out_shape=shape(KV_HEADS, GROUP + 2, PIECE, HEAD_DIM),
        in_specs=[HBM, HBM, HBM],
        out_specs=VMEM,
        scratch_shapes=[pltpu.SemaphoreType.DMA((KV_HEADS, GROUP + 2))],
        name="pack",
    )(q, k, v)


def fan(packed):
    return pl.pallas_call(
        fan_kernel,
        out_shape=shape(16, SOURCES, 2, PIECE, HEAD_DIM),
        in_specs=[VMEM],
        out_specs=VMEM,
        compiler_params=SMALL,
        name="fan",
    )(packed)


SWAP = [(0, 1), (1, 0)]
PLANE = [
    [((ylo * 2 + core) * 2 + yhi) * 4 + x for ylo in range(2) for yhi in range(2) for x in range(4)]
    for core in range(2)
]


def look(values, at):
    index = jnp.arange(values.shape[0], dtype=jnp.int32)
    return jnp.sum(jnp.where(at[:, None] == index[None, :], values[None, :], 0), axis=1)


def table(visit_ids, span_order):
    zlo = lax.axis_index("zlo").astype(jnp.int32)
    block = jnp.arange(SPANS, dtype=jnp.int32)
    mine = (block // 4) % 2 == zlo
    upto = jnp.arange(SPANS + 1, dtype=jnp.int32)
    count = jnp.sum(
        (mine[None, :] & (span_order[None, :] < upto[:, None])).astype(jnp.int32), axis=1
    )
    ranks = jnp.arange(HALF, dtype=jnp.int32)
    ordered = jnp.sum((count[None, 1:] <= ranks[:, None]).astype(jnp.int32), axis=1)
    starts = jnp.sum(
        (visit_ids[None, :] < jnp.arange(VISITS, dtype=jnp.int32)[:, None]).astype(jnp.int32),
        axis=1,
    )
    at = lax.axis_index("plane")
    place = jnp.stack([at // 16, at // 8 % 2, zlo, at % 8 * PIECE]).astype(jnp.int32)
    lists, totals = [], []
    for side in (zlo, 1 - zlo):
        source = (jnp.arange(SOURCES, dtype=jnp.int32) * 2 + side) * 4 + place[0] * 2 + place[1]
        span = look(span_order, source)
        p0 = span * SPAN_ROWS + place[3]
        low = jnp.max(jnp.where(starts[None, :] <= p0[:, None], starts[None, :], 0), axis=1)
        tile_a = look(count, low // SPAN_ROWS) // PER_TILE
        tile_b = (look(count, span + 1) + PER_TILE - 1) // PER_TILE
        size = jnp.maximum(tile_b - tile_a, 0)
        order = jnp.arange(SOURCES)
        ends = jnp.sum(jnp.where(order[None, :] <= order[:, None], size[None, :], 0), axis=1)
        at = jnp.arange(ITEMS, dtype=jnp.int32)
        slot = jnp.sum((ends[None, :] <= at[:, None]).astype(jnp.int32), axis=1)
        tile = at + look(tile_a - ends + size, slot)
        lists.append(slot * 16 + jnp.where(slot < SOURCES, tile, 0))
        totals.append(jnp.sum(size)[None])
    return jnp.concatenate([span_order, count, ordered, starts, place] + totals + lists)


def body(queries, key_rows, value_rows, visit_ids, span_order):
    info = table(visit_ids, span_order)
    packed = pack(queries, key_rows, value_rows)
    packed = lax.all_to_all(packed, "zhi", 0, 0, tiled=True)
    far_q = lax.ppermute(packed, "zlo", SWAP)
    spread = fan(packed)
    own = lax.all_to_all(
        spread, "plane", 0, 0, axis_index_groups=PLANE, tiled=True
    )
    other = lax.ppermute(own, "plane", [(i, i ^ 8) for i in range(32)])
    k, v = order_part(info, own)

    far_out, k, v = far_part(info, far_q, other, k, v)
    sent = lax.ppermute(far_out, "zlo", SWAP)
    near_out, mass = near_part(info, packed, k, v)
    out = merge(near_out, mass, sent)
    out = lax.all_to_all(out, "zhi", 0, 0, tiled=True)
    return jnp.transpose(out, (1, 0, 2)).reshape(PIECE, HEADS * HEAD_DIM)


def solution(mesh):
    fine = Mesh(mesh.devices.reshape(8, 2, 32), ("zhi", "zlo", "plane"))
    rows = P(("zhi", "zlo", "plane"), None)
    return jax.shard_map(
        body,
        mesh=fine,
        in_specs=(rows, rows, rows, P(), P()),
        out_specs=rows,
        check_vma=False,
    )
```

```python
import jax
import jax.numpy as jnp
from jax import lax
from jax.experimental import pallas as pl
from jax.experimental.pallas import tpu as pltpu
from jax.sharding import Mesh, PartitionSpec as P

HEADS = 32
KV_HEADS = 8
HEAD_DIM = 128
GROUP = HEADS // KV_HEADS
SPAN_ROWS = 192
PIECE = 24
PARTS = SPAN_ROWS // PIECE
VISITS = 4
SPANS = 64
HALF = SPANS // 2
KEYS = HALF * SPAN_ROWS
PER_TILE = 4
UNROLL = 3
TILE = PER_TILE * SPAN_ROWS
TILES = KEYS // TILE
SOURCES = 8
ROWS = GROUP * PIECE
SCALE_LOG2 = HEAD_DIM ** (-0.5) * 1.4426950408889634
NOTHING = -3e38

ORDER = 0
COUNT = 64
SORTED = COUNT + 65
START = SORTED + HALF
YLO = START + VISITS
CORE = YLO + 1
ZLO = YLO + 2
FIRST = YLO + 3
TOTAL = YLO + 4
LIST = TOTAL + 2
ITEMS = SOURCES // 2 * TILES + UNROLL


def take_keys(info, src, side, k_buf, v_buf):
    zlo = info[ZLO]
    pieces = [buf.reshape(HALF * PARTS, PIECE, HEAD_DIM) for buf in (k_buf, v_buf)]

    def step(i, carry):
        k, half = i // 2, i % 2
        span = info[ORDER + (k * 2 + zlo) * 4 + half * 2 + side]
        rank = info[COUNT + span]
        for part in range(PARTS):
            for which, buf in enumerate(pieces):
                buf[rank * PARTS + part] = src[half * PARTS + part, k, which]
        return carry

    lax.fori_loop(0, 2 * SOURCES, step, 0)


def attend_sources(info, side, q_ref, k_buf, v_buf, scratch, put):
    s_buf, q_buf, low_buf, pos_buf, best, top_buf, total, acc = scratch
    ylo, core, first = info[YLO], info[CORE], info[FIRST]
    inside = lax.broadcasted_iota(jnp.int32, (PIECE, HEAD_DIM), 0)
    lane = lax.broadcasted_iota(jnp.int32, (1, HEAD_DIM), 1)

    def start_of(pos):
        low = jnp.zeros_like(pos)
        for v in range(1, VISITS):
            low = jnp.where(info[START + v] <= pos, info[START + v], low)
        return low

    for n in range(SOURCES):
        span = info[ORDER + (n * 2 + side) * 4 + ylo * 2 + core]
        pos = span * SPAN_ROWS + first + inside
        pos_buf[n] = pos
        low_buf[n] = start_of(pos)
        q_buf[n] = (
            q_ref[n].astype(jnp.float32).reshape(ROWS, HEAD_DIM).astype(jnp.bfloat16)
        )
        best[n] = jnp.full((ROWS, HEAD_DIM), -jnp.inf, jnp.float32)
        total[n] = jnp.zeros((ROWS, HEAD_DIM), jnp.float32)
        acc[n] = jnp.zeros((ROWS, HEAD_DIM), jnp.float32)
    far = jnp.where(side == info[ZLO], 0, 1)
    steps = (info[TOTAL + far] + UNROLL - 1) // UNROLL
    listed = LIST + far * ITEMS

    def item(at):
        entry = info[listed + at]
        return (entry // 256, entry // 16 % 16), entry % 16

    def scores(i, carry):
        for u in range(UNROLL):
            at = i * UNROLL + u
            slots, j = item(at)
            sources = [jnp.minimum(slot, SOURCES - 1) for slot in slots]
            both = lax.dot_general(
                jnp.concatenate([q_buf[n] for n in sources], axis=0),
                k_buf[pl.ds(pl.multiple_of(j * TILE, TILE), TILE), :],
                (((1,), (1,)), ((), ())),
                preferred_element_type=jnp.float32,
            )
            base = [
                (info[SORTED + j * PER_TILE + w] - w) * SPAN_ROWS for w in range(PER_TILE)
            ]
            keys = []
            for c in range(TILE // HEAD_DIM):
                left = c * HEAD_DIM // SPAN_ROWS
                right = (c * HEAD_DIM + HEAD_DIM - 1) // SPAN_ROWS
                key = lane + c * HEAD_DIM
                if left == right:
                    key = key + base[left]
                else:
                    key = key + jnp.where(key < right * SPAN_ROWS, base[left], base[right])
                keys.append(key)
            for e in range(2):
                s = both[e * ROWS : (e + 1) * ROWS].reshape(GROUP, PIECE, TILE)
                low, pos = low_buf[sources[e]], pos_buf[sources[e]]
                high = best[slots[e]].reshape(GROUP, PIECE, HEAD_DIM)
                for c, key in enumerate(keys):
                    keep = (key >= low) & (key <= pos)
                    part = jnp.where(
                        keep[None], s[:, :, c * HEAD_DIM : (c + 1) * HEAD_DIM], -jnp.inf
                    )
                    s_buf[
                        at,
                        e * ROWS : (e + 1) * ROWS,
                        c * HEAD_DIM : (c + 1) * HEAD_DIM,
                    ] = part.reshape(ROWS, HEAD_DIM)
                    high = jnp.maximum(high, part)
                best[slots[e]] = high.reshape(ROWS, HEAD_DIM)
        return carry

    lax.fori_loop(0, steps, scores, 0)

    for n in range(SOURCES):
        top = jnp.max(best[n], axis=1, keepdims=True)
        top_buf[n] = jnp.broadcast_to(top, (ROWS, HEAD_DIM))

    def mix(i, carry):
        for u in range(UNROLL):
            at = i * UNROLL + u
            slots, j = item(at)
            rows = []
            for e in range(2):
                top = top_buf[jnp.minimum(slots[e], SOURCES - 1)]
                top = jnp.where(top > -jnp.inf, top, 0.0)
                part_sum = total[slots[e]]
                parts = []
                for c in range(TILE // HEAD_DIM):
                    part = s_buf[
                        at,
                        e * ROWS : (e + 1) * ROWS,
                        c * HEAD_DIM : (c + 1) * HEAD_DIM,
                    ]
                    w = jnp.exp2((part - top) * SCALE_LOG2)
                    part_sum = part_sum + w
                    parts.append(w.astype(jnp.bfloat16))
                total[slots[e]] = part_sum
                rows.append(jnp.concatenate(parts, axis=1))
            mixed = jnp.dot(
                jnp.concatenate(rows, axis=0),
                v_buf[pl.ds(pl.multiple_of(j * TILE, TILE), TILE), :],
                preferred_element_type=jnp.float32,
            )
            for e in range(2):
                acc[slots[e]] = acc[slots[e]] + mixed[e * ROWS : (e + 1) * ROWS]
        return carry

    lax.fori_loop(0, steps, mix, 0)

    for n in range(SOURCES):
        top = top_buf[n]
        whole, out = jnp.sum(total[n], axis=1, keepdims=True), acc[n]
        some = top > -jnp.inf
        safe = jnp.where(some, whole, 1.0)
        mass = jnp.where(some, top * SCALE_LOG2 + jnp.log2(safe), NOTHING)
        put(
            n,
            (out / safe).reshape(GROUP, PIECE, HEAD_DIM),
            mass.reshape(GROUP, PIECE, HEAD_DIM),
        )


def order_kernel(info, own_ref, k_buf, v_buf):
    take_keys(info, own_ref, info[CORE], k_buf, v_buf)


def far_kernel(info, q_ref, other_ref, k_half, v_half, o_ref, k_buf, v_buf, *scratch):
    take_keys(info, other_ref, 1 - info[CORE], k_buf, v_buf)
    lane = lax.broadcasted_iota(jnp.int32, (PIECE, HEAD_DIM), 1)

    def put(n, out, mass):
        o_ref[n, :GROUP] = out.astype(jnp.bfloat16)
        high = mass.astype(jnp.bfloat16).astype(jnp.float32)
        rest = mass - high
        middle = rest.astype(jnp.bfloat16).astype(jnp.float32)
        pieces = (high, middle, rest - middle)
        packed = jnp.zeros((PIECE, HEAD_DIM), jnp.float32)
        for g in range(GROUP):
            for i, piece in enumerate(pieces):
                packed = jnp.where(lane == 3 * g + i, piece[g], packed)
        o_ref[n, GROUP] = packed.astype(jnp.bfloat16)

    attend_sources(info, 1 - info[ZLO], q_ref, k_buf, v_buf, scratch, put)


def near_kernel(info, q_ref, k_buf, v_buf, o_ref, m_ref, *scratch):
    def put(n, out, mass):
        o_ref[n] = out
        m_ref[n] = mass

    attend_sources(info, info[ZLO], q_ref, k_buf, v_buf, scratch, put)


def merge_kernel(near_ref, mass_ref, far_ref, o_ref):
    for n in range(SOURCES):
        packed = far_ref[n, GROUP].astype(jnp.float32)
        for g in range(GROUP):
            a = mass_ref[n, g]
            b = (
                packed[:, 3 * g : 3 * g + 1]
                + packed[:, 3 * g + 1 : 3 * g + 2]
                + packed[:, 3 * g + 2 : 3 * g + 3]
            )
            m = jnp.maximum(a, b)
            wa, wb = jnp.exp2(a - m), jnp.exp2(b - m)
            out = (wa * near_ref[n, g] + wb * far_ref[n, g].astype(jnp.float32)) / (wa + wb)
            o_ref[n, :, g * HEAD_DIM : (g + 1) * HEAD_DIM] = out.astype(jnp.bfloat16)


def pack_kernel(q_ref, k_ref, v_ref, o_ref):
    for h in range(KV_HEADS):
        o_ref[h, 0] = k_ref[:, h * HEAD_DIM : (h + 1) * HEAD_DIM]
        o_ref[h, 1] = v_ref[:, h * HEAD_DIM : (h + 1) * HEAD_DIM]
        for g in range(GROUP):
            c = (h * GROUP + g) * HEAD_DIM
            o_ref[h, 2 + g] = q_ref[:, c : c + HEAD_DIM]


def fan_kernel(packed_ref, o_ref, q_ref):
    for i in range(16):
        o_ref[i] = packed_ref[:, :2]
    q_ref[...] = packed_ref[:, 2:]


SMEM = pl.BlockSpec(memory_space=pltpu.SMEM)
VMEM = pl.BlockSpec(memory_space=pltpu.VMEM)
COST = pl.CostEstimate(flops=6_000_000_000, bytes_accessed=4_000_000, transcendentals=4_000_000)


def shape(*sizes, kind=jnp.bfloat16):
    return jax.ShapeDtypeStruct(sizes, kind)


SCRATCH = [
    pltpu.VMEM((ITEMS, 2 * ROWS, TILE), jnp.float32),
    pltpu.VMEM((SOURCES, ROWS, HEAD_DIM), jnp.bfloat16),
    pltpu.VMEM((SOURCES, PIECE, HEAD_DIM), jnp.int32),
    pltpu.VMEM((SOURCES, PIECE, HEAD_DIM), jnp.int32),
    pltpu.VMEM((SOURCES + 1, ROWS, HEAD_DIM), jnp.float32),
    pltpu.VMEM((SOURCES, ROWS, HEAD_DIM), jnp.float32),
    pltpu.VMEM((SOURCES + 1, ROWS, HEAD_DIM), jnp.float32),
    pltpu.VMEM((SOURCES + 1, ROWS, HEAD_DIM), jnp.float32),
]
SMALL = pltpu.CompilerParams(vmem_limit_bytes=8 << 20)
LIMIT = pltpu.CompilerParams(vmem_limit_bytes=40 << 20)


def order_part(info, own):
    return pl.pallas_call(
        order_kernel,
        out_shape=(shape(KEYS, HEAD_DIM), shape(KEYS, HEAD_DIM)),
        in_specs=[SMEM, VMEM],
        out_specs=(VMEM, VMEM),
        compiler_params=SMALL,
        cost_estimate=pl.CostEstimate(flops=0, bytes_accessed=6_000_000, transcendentals=0),
        name="order",
    )(info, own)


def far_part(info, q, other, k, v):
    return pl.pallas_call(
        far_kernel,
        out_shape=(
            shape(SOURCES, GROUP + 1, PIECE, HEAD_DIM),
            shape(KEYS, HEAD_DIM),
            shape(KEYS, HEAD_DIM),
        ),
        in_specs=[SMEM, VMEM, VMEM, VMEM, VMEM],
        out_specs=(VMEM, VMEM, VMEM),
        scratch_shapes=SCRATCH,
        input_output_aliases={3: 1, 4: 2},
        compiler_params=LIMIT,
        cost_estimate=COST,
        name="far",
    )(info, q, other, k, v)


def near_part(info, q, k, v):
    return pl.pallas_call(
        near_kernel,
        out_shape=(
            shape(SOURCES, GROUP, PIECE, HEAD_DIM, kind=jnp.float32),
            shape(SOURCES, GROUP, PIECE, HEAD_DIM, kind=jnp.float32),
        ),
        in_specs=[SMEM, VMEM, VMEM, VMEM],
        out_specs=(VMEM, VMEM),
        scratch_shapes=SCRATCH,
        compiler_params=LIMIT,
        cost_estimate=COST,
        name="near",
    )(info, q, k, v)


def merge(near, mass, far):
    return pl.pallas_call(
        merge_kernel,
        out_shape=shape(SOURCES, PIECE, GROUP * HEAD_DIM),
        in_specs=[VMEM, VMEM, VMEM],
        out_specs=VMEM,
        compiler_params=SMALL,
        name="merge",
    )(near, mass, far)


def pack(q, k, v):
    return pl.pallas_call(
        pack_kernel,
        out_shape=shape(KV_HEADS, GROUP + 2, PIECE, HEAD_DIM),
        in_specs=[VMEM, VMEM, VMEM],
        out_specs=VMEM,
        name="pack",
    )(q, k, v)


def fan(packed):
    return pl.pallas_call(
        fan_kernel,
        out_shape=(
            shape(16, SOURCES, 2, PIECE, HEAD_DIM),
            shape(SOURCES, GROUP, PIECE, HEAD_DIM),
        ),
        in_specs=[VMEM],
        out_specs=(VMEM, VMEM),
        compiler_params=SMALL,
        name="fan",
    )(packed)


SWAP = [(0, 1), (1, 0)]
PLANE = [
    [((ylo * 2 + core) * 2 + yhi) * 4 + x for ylo in range(2) for yhi in range(2) for x in range(4)]
    for core in range(2)
]


def look(values, at):
    index = jnp.arange(values.shape[0], dtype=jnp.int32)
    return jnp.sum(jnp.where(at[:, None] == index[None, :], values[None, :], 0), axis=1)


def table(visit_ids, span_order):
    zlo = lax.axis_index("zlo").astype(jnp.int32)
    block = jnp.arange(SPANS, dtype=jnp.int32)
    mine = (block // 4) % 2 == zlo
    upto = jnp.arange(SPANS + 1, dtype=jnp.int32)
    count = jnp.sum(
        (mine[None, :] & (span_order[None, :] < upto[:, None])).astype(jnp.int32), axis=1
    )
    ranks = jnp.arange(HALF, dtype=jnp.int32)
    ordered = jnp.sum((count[None, 1:] <= ranks[:, None]).astype(jnp.int32), axis=1)
    starts = jnp.sum(
        (visit_ids[None, :] < jnp.arange(VISITS, dtype=jnp.int32)[:, None]).astype(jnp.int32),
        axis=1,
    )
    at = lax.axis_index("plane")
    place = jnp.stack([at // 16, at // 8 % 2, zlo, at % 8 * PIECE]).astype(jnp.int32)
    side = jnp.stack([zlo, 1 - zlo])[:, None]
    source = (jnp.arange(SOURCES, dtype=jnp.int32)[None] * 2 + side) * 4
    span = look(span_order, source.reshape(-1) + place[0] * 2 + place[1])
    p0 = span * SPAN_ROWS + place[3]
    low = jnp.max(jnp.where(starts[None, :] <= p0[:, None], starts[None, :], 0), axis=1)
    tile_a = look(count, low // SPAN_ROWS) // PER_TILE
    tile_b = (look(count, span + 1) + PER_TILE - 1) // PER_TILE
    tiles = jnp.arange(TILES, dtype=jnp.int32)
    active = (tile_a[:, None] <= tiles) & (tiles < tile_b[:, None])
    active = active.reshape(2, SOURCES, TILES).astype(jnp.int32)
    n = jnp.arange(SOURCES, dtype=jnp.int32)
    before = (n[None, :] < n[:, None]).astype(jnp.int32)
    rank = jnp.sum(before[None, :, :, None] * active[:, None], axis=2)
    pairs = (jnp.sum(active, axis=1) + 1) // 2
    earlier = (tiles[None, :] < tiles[:, None]).astype(jnp.int32)
    offset = jnp.sum(earlier[None] * pairs[:, None, :], axis=2)
    at = jnp.arange(ITEMS, dtype=jnp.int32)
    where = jnp.where(active == 1, offset[:, None, :] * 2 + rank, -1)
    where = where.reshape(2, 1, SOURCES * TILES)
    owner = jnp.repeat(n, TILES)[None, None] - SOURCES

    def owners(half):
        hit = where == (at * 2 + half)[None, :, None]
        return SOURCES + jnp.sum(jnp.where(hit, owner, 0), axis=2)

    done = (offset + pairs)[:, None, :] <= at[None, :, None]
    tile = jnp.minimum(jnp.sum(done.astype(jnp.int32), axis=2), TILES - 1)
    listed = owners(0) * 256 + owners(1) * 16 + tile
    return jnp.concatenate(
        [span_order, count, ordered, starts, place, jnp.sum(pairs, axis=1), listed.reshape(-1)]
    )


def body(queries, key_rows, value_rows, visit_ids, span_order):
    info = table(visit_ids, span_order)
    packed = pack(queries, key_rows, value_rows)
    packed = lax.all_to_all(packed, "zhi", 0, 0, tiled=True)
    spread, near_q = fan(packed)
    own = lax.all_to_all(
        spread, "plane", 0, 0, axis_index_groups=PLANE, tiled=True
    )
    far_q = lax.ppermute(near_q, "zlo", SWAP)
    other = lax.ppermute(own, "plane", [(i, i ^ 8) for i in range(32)])
    k, v = order_part(info, own)

    far_out, k, v = far_part(info, far_q, other, k, v)
    sent = lax.ppermute(far_out, "zlo", SWAP)
    near_out, mass = near_part(info, near_q, k, v)
    out = merge(near_out, mass, sent)
    out = lax.all_to_all(out, "zhi", 0, 0, tiled=True)
    return jnp.transpose(out, (1, 0, 2)).reshape(PIECE, HEADS * HEAD_DIM)


def solution(mesh):
    fine = Mesh(mesh.devices.reshape(8, 2, 32), ("zhi", "zlo", "plane"))
    rows = P(("zhi", "zlo", "plane"), None)
    return jax.shard_map(
        body,
        mesh=fine,
        in_specs=(rows, rows, rows, P(), P()),
        out_specs=rows,
        check_vma=False,
    )
```

```python
import jax
import jax.numpy as jnp
from jax import lax
from jax.experimental import pallas as pl
from jax.experimental.pallas import tpu as pltpu
from jax.sharding import Mesh, PartitionSpec as P

HEADS = 32
KV_HEADS = 8
HEAD_DIM = 128
GROUP = HEADS // KV_HEADS
SPAN_ROWS = 192
PIECE = 24
PARTS = SPAN_ROWS // PIECE
VISITS = 4
SPANS = 64
HALF = SPANS // 2
KEYS = HALF * SPAN_ROWS
PER_TILE = 4
UNROLL = 3
TILE = PER_TILE * SPAN_ROWS
TILES = KEYS // TILE
SOURCES = 8
ROWS = GROUP * PIECE
SCALE_LOG2 = HEAD_DIM ** (-0.5) * 1.4426950408889634
NOTHING = -3e38

ORDER = 0
COUNT = 64
SORTED = COUNT + 65
START = SORTED + HALF
YLO = START + VISITS
CORE = YLO + 1
ZLO = YLO + 2
FIRST = YLO + 3
TOTAL = YLO + 4
LIST = TOTAL + 2
ITEMS = SOURCES // 2 * TILES + UNROLL


def take_keys(info, src, side, k_buf, v_buf):
    zlo = info[ZLO]
    pieces = [buf.reshape(HALF * PARTS, PIECE, HEAD_DIM) for buf in (k_buf, v_buf)]

    def step(i, carry):
        k, half = i // 2, i % 2
        span = info[ORDER + (k * 2 + zlo) * 4 + half * 2 + side]
        rank = info[COUNT + span]
        for part in range(PARTS):
            for which, buf in enumerate(pieces):
                buf[rank * PARTS + part] = src[half * PARTS + part, k, which]
        return carry

    lax.fori_loop(0, 2 * SOURCES, step, 0)


def attend_sources(info, side, q_ref, k_buf, v_buf, scratch, put):
    s_buf, q_buf, low_buf, pos_buf, best, top_buf, total, acc = scratch
    ylo, core, first = info[YLO], info[CORE], info[FIRST]
    inside = lax.broadcasted_iota(jnp.int32, (PIECE, HEAD_DIM), 0)
    lane = lax.broadcasted_iota(jnp.int32, (1, HEAD_DIM), 1)

    def start_of(pos):
        low = jnp.zeros_like(pos)
        for v in range(1, VISITS):
            low = jnp.where(info[START + v] <= pos, info[START + v], low)
        return low

    for n in range(SOURCES):
        span = info[ORDER + (n * 2 + side) * 4 + ylo * 2 + core]
        pos = span * SPAN_ROWS + first + inside
        pos_buf[n] = pos
        low_buf[n] = start_of(pos)
        q_buf[n] = (
            q_ref[n].astype(jnp.float32).reshape(ROWS, HEAD_DIM).astype(jnp.bfloat16)
        )
        best[n] = jnp.full((ROWS, HEAD_DIM), -jnp.inf, jnp.float32)
        total[n] = jnp.zeros((ROWS, HEAD_DIM), jnp.float32)
        acc[n] = jnp.zeros((ROWS, HEAD_DIM), jnp.float32)
    far = jnp.where(side == info[ZLO], 0, 1)
    steps = (info[TOTAL + far] + UNROLL - 1) // UNROLL
    listed = LIST + far * ITEMS

    def item(at):
        entry = info[listed + at]
        return (entry // 256, entry // 16 % 16), entry % 16

    def scores(i, carry):
        for u in range(UNROLL):
            at = i * UNROLL + u
            slots, j = item(at)
            sources = [jnp.minimum(slot, SOURCES - 1) for slot in slots]
            both = lax.dot_general(
                jnp.concatenate([q_buf[n] for n in sources], axis=0),
                k_buf[pl.ds(pl.multiple_of(j * TILE, TILE), TILE), :],
                (((1,), (1,)), ((), ())),
                preferred_element_type=jnp.float32,
            )
            base = [
                (info[SORTED + j * PER_TILE + w] - w) * SPAN_ROWS for w in range(PER_TILE)
            ]
            keys = []
            for c in range(TILE // HEAD_DIM):
                left = c * HEAD_DIM // SPAN_ROWS
                right = (c * HEAD_DIM + HEAD_DIM - 1) // SPAN_ROWS
                key = lane + c * HEAD_DIM
                if left == right:
                    key = key + base[left]
                else:
                    key = key + jnp.where(key < right * SPAN_ROWS, base[left], base[right])
                keys.append(key)
            for e in range(2):
                s = both[e * ROWS : (e + 1) * ROWS].reshape(GROUP, PIECE, TILE)
                low, pos = low_buf[sources[e]], pos_buf[sources[e]]
                high = best[slots[e]].reshape(GROUP, PIECE, HEAD_DIM)
                for c, key in enumerate(keys):
                    keep = (key >= low) & (key <= pos)
                    part = jnp.where(
                        keep[None], s[:, :, c * HEAD_DIM : (c + 1) * HEAD_DIM], -jnp.inf
                    )
                    s_buf[
                        at,
                        e * ROWS : (e + 1) * ROWS,
                        c * HEAD_DIM : (c + 1) * HEAD_DIM,
                    ] = part.reshape(ROWS, HEAD_DIM)
                    high = jnp.maximum(high, part)
                best[slots[e]] = high.reshape(ROWS, HEAD_DIM)
        return carry

    lax.fori_loop(0, steps, scores, 0)

    for n in range(SOURCES):
        top = jnp.max(best[n], axis=1, keepdims=True)
        top_buf[n] = jnp.broadcast_to(top, (ROWS, HEAD_DIM))

    def mix(i, carry):
        for u in range(UNROLL):
            at = i * UNROLL + u
            slots, j = item(at)
            rows = []
            for e in range(2):
                top = top_buf[jnp.minimum(slots[e], SOURCES - 1)]
                top = jnp.where(top > -jnp.inf, top, 0.0)
                part_sum = total[slots[e]]
                parts = []
                for c in range(TILE // HEAD_DIM):
                    part = s_buf[
                        at,
                        e * ROWS : (e + 1) * ROWS,
                        c * HEAD_DIM : (c + 1) * HEAD_DIM,
                    ]
                    w = jnp.exp2((part - top) * SCALE_LOG2)
                    part_sum = part_sum + w
                    parts.append(w.astype(jnp.bfloat16))
                total[slots[e]] = part_sum
                rows.append(jnp.concatenate(parts, axis=1))
            mixed = jnp.dot(
                jnp.concatenate(rows, axis=0),
                v_buf[pl.ds(pl.multiple_of(j * TILE, TILE), TILE), :],
                preferred_element_type=jnp.float32,
            )
            for e in range(2):
                acc[slots[e]] = acc[slots[e]] + mixed[e * ROWS : (e + 1) * ROWS]
        return carry

    lax.fori_loop(0, steps, mix, 0)

    for n in range(SOURCES):
        top = top_buf[n]
        whole, out = jnp.sum(total[n], axis=1, keepdims=True), acc[n]
        some = top > -jnp.inf
        safe = jnp.where(some, whole, 1.0)
        mass = jnp.where(some, top * SCALE_LOG2 + jnp.log2(safe), NOTHING)
        put(
            n,
            (out / safe).reshape(GROUP, PIECE, HEAD_DIM),
            mass.reshape(GROUP, PIECE, HEAD_DIM),
        )


def order_kernel(info, own_ref, k_buf, v_buf):
    take_keys(info, own_ref, info[CORE], k_buf, v_buf)


def far_kernel(info, q_ref, other_ref, k_half, v_half, o_ref, k_buf, v_buf, *scratch):
    take_keys(info, other_ref, 1 - info[CORE], k_buf, v_buf)
    lane = lax.broadcasted_iota(jnp.int32, (PIECE, HEAD_DIM), 1)

    packed = [jnp.zeros((PIECE, HEAD_DIM), jnp.float32)]

    def put(n, out, mass):
        o_ref[n * GROUP : (n + 1) * GROUP] = out.astype(jnp.bfloat16)
        high = mass.astype(jnp.bfloat16).astype(jnp.float32)
        rest = mass - high
        middle = rest.astype(jnp.bfloat16).astype(jnp.float32)
        for i, piece in enumerate((high, middle, rest - middle)):
            for g in range(GROUP):
                packed[0] = jnp.where(
                    lane == (n * GROUP + g) * 3 + i, piece[g], packed[0]
                )

    attend_sources(info, 1 - info[ZLO], q_ref, k_buf, v_buf, scratch, put)
    o_ref[SOURCES * GROUP] = packed[0].astype(jnp.bfloat16)


def near_kernel(info, q_ref, k_buf, v_buf, o_ref, m_ref, *scratch):
    def put(n, out, mass):
        o_ref[n] = out
        m_ref[n] = mass

    attend_sources(info, info[ZLO], q_ref, k_buf, v_buf, scratch, put)


def merge_kernel(near_ref, mass_ref, far_ref, o_ref):
    packed = far_ref[SOURCES * GROUP].astype(jnp.float32)
    for n in range(SOURCES):
        for g in range(GROUP):
            c = (n * GROUP + g) * 3
            a = mass_ref[n, g]
            b = (
                packed[:, c : c + 1] + packed[:, c + 1 : c + 2] + packed[:, c + 2 : c + 3]
            )
            m = jnp.maximum(a, b)
            wa, wb = jnp.exp2(a - m), jnp.exp2(b - m)
            out = (wa * near_ref[n, g] + wb * far_ref[n * GROUP + g].astype(jnp.float32)) / (wa + wb)
            o_ref[n, :, g * HEAD_DIM : (g + 1) * HEAD_DIM] = out.astype(jnp.bfloat16)


def pack_kernel(q_ref, k_ref, v_ref, o_ref):
    for h in range(KV_HEADS):
        o_ref[h, 0] = k_ref[:, h * HEAD_DIM : (h + 1) * HEAD_DIM]
        o_ref[h, 1] = v_ref[:, h * HEAD_DIM : (h + 1) * HEAD_DIM]
        for g in range(GROUP):
            c = (h * GROUP + g) * HEAD_DIM
            o_ref[h, 2 + g] = q_ref[:, c : c + HEAD_DIM]


def fan_kernel(packed_ref, o_ref, q_ref):
    for i in range(16):
        o_ref[i] = packed_ref[:, :2]
    q_ref[...] = packed_ref[:, 2:]


SMEM = pl.BlockSpec(memory_space=pltpu.SMEM)
VMEM = pl.BlockSpec(memory_space=pltpu.VMEM)
COST = pl.CostEstimate(flops=6_000_000_000, bytes_accessed=4_000_000, transcendentals=4_000_000)


def shape(*sizes, kind=jnp.bfloat16):
    return jax.ShapeDtypeStruct(sizes, kind)


SCRATCH = [
    pltpu.VMEM((ITEMS, 2 * ROWS, TILE), jnp.float32),
    pltpu.VMEM((SOURCES, ROWS, HEAD_DIM), jnp.bfloat16),
    pltpu.VMEM((SOURCES, PIECE, HEAD_DIM), jnp.int32),
    pltpu.VMEM((SOURCES, PIECE, HEAD_DIM), jnp.int32),
    pltpu.VMEM((SOURCES + 1, ROWS, HEAD_DIM), jnp.float32),
    pltpu.VMEM((SOURCES, ROWS, HEAD_DIM), jnp.float32),
    pltpu.VMEM((SOURCES + 1, ROWS, HEAD_DIM), jnp.float32),
    pltpu.VMEM((SOURCES + 1, ROWS, HEAD_DIM), jnp.float32),
]
SMALL = pltpu.CompilerParams(vmem_limit_bytes=8 << 20)
LIMIT = pltpu.CompilerParams(vmem_limit_bytes=40 << 20)


def order_part(info, own):
    return pl.pallas_call(
        order_kernel,
        out_shape=(shape(KEYS, HEAD_DIM), shape(KEYS, HEAD_DIM)),
        in_specs=[SMEM, VMEM],
        out_specs=(VMEM, VMEM),
        compiler_params=SMALL,
        cost_estimate=pl.CostEstimate(flops=0, bytes_accessed=6_000_000, transcendentals=0),
        name="order",
    )(info, own)


def far_part(info, q, other, k, v):
    return pl.pallas_call(
        far_kernel,
        out_shape=(
            shape(SOURCES * GROUP + 1, PIECE, HEAD_DIM),
            shape(KEYS, HEAD_DIM),
            shape(KEYS, HEAD_DIM),
        ),
        in_specs=[SMEM, VMEM, VMEM, VMEM, VMEM],
        out_specs=(VMEM, VMEM, VMEM),
        scratch_shapes=SCRATCH,
        input_output_aliases={3: 1, 4: 2},
        compiler_params=LIMIT,
        cost_estimate=COST,
        name="far",
    )(info, q, other, k, v)


def near_part(info, q, k, v):
    return pl.pallas_call(
        near_kernel,
        out_shape=(
            shape(SOURCES, GROUP, PIECE, HEAD_DIM, kind=jnp.float32),
            shape(SOURCES, GROUP, PIECE, HEAD_DIM, kind=jnp.float32),
        ),
        in_specs=[SMEM, VMEM, VMEM, VMEM],
        out_specs=(VMEM, VMEM),
        scratch_shapes=SCRATCH,
        compiler_params=LIMIT,
        cost_estimate=COST,
        name="near",
    )(info, q, k, v)


def merge(near, mass, far):
    return pl.pallas_call(
        merge_kernel,
        out_shape=shape(SOURCES, PIECE, GROUP * HEAD_DIM),
        in_specs=[VMEM, VMEM, VMEM],
        out_specs=VMEM,
        compiler_params=SMALL,
        name="merge",
    )(near, mass, far)


def pack(q, k, v):
    return pl.pallas_call(
        pack_kernel,
        out_shape=shape(KV_HEADS, GROUP + 2, PIECE, HEAD_DIM),
        in_specs=[VMEM, VMEM, VMEM],
        out_specs=VMEM,
        name="pack",
    )(q, k, v)


def fan(packed):
    return pl.pallas_call(
        fan_kernel,
        out_shape=(
            shape(16, SOURCES, 2, PIECE, HEAD_DIM),
            shape(SOURCES, GROUP, PIECE, HEAD_DIM),
        ),
        in_specs=[VMEM],
        out_specs=(VMEM, VMEM),
        compiler_params=SMALL,
        name="fan",
    )(packed)


SWAP = [(0, 1), (1, 0)]
PLANE = [
    [((ylo * 2 + core) * 2 + yhi) * 4 + x for ylo in range(2) for yhi in range(2) for x in range(4)]
    for core in range(2)
]


def look(values, at):
    index = jnp.arange(values.shape[0], dtype=jnp.int32)
    return jnp.sum(jnp.where(at[:, None] == index[None, :], values[None, :], 0), axis=1)


def table(visit_ids, span_order):
    zlo = lax.axis_index("zlo").astype(jnp.int32)
    block = jnp.arange(SPANS, dtype=jnp.int32)
    mine = (block // 4) % 2 == zlo
    upto = jnp.arange(SPANS + 1, dtype=jnp.int32)
    count = jnp.sum(
        (mine[None, :] & (span_order[None, :] < upto[:, None])).astype(jnp.int32), axis=1
    )
    ranks = jnp.arange(HALF, dtype=jnp.int32)
    ordered = jnp.sum((count[None, 1:] <= ranks[:, None]).astype(jnp.int32), axis=1)
    starts = jnp.sum(
        (visit_ids[None, :] < jnp.arange(VISITS, dtype=jnp.int32)[:, None]).astype(jnp.int32),
        axis=1,
    )
    at = lax.axis_index("plane")
    place = jnp.stack([at // 16, at // 8 % 2, zlo, at % 8 * PIECE]).astype(jnp.int32)
    side = jnp.stack([zlo, 1 - zlo])[:, None]
    source = (jnp.arange(SOURCES, dtype=jnp.int32)[None] * 2 + side) * 4
    span = look(span_order, source.reshape(-1) + place[0] * 2 + place[1])
    p0 = span * SPAN_ROWS + place[3]
    low = jnp.max(jnp.where(starts[None, :] <= p0[:, None], starts[None, :], 0), axis=1)
    tile_a = look(count, low // SPAN_ROWS) // PER_TILE
    tile_b = (look(count, span + 1) + PER_TILE - 1) // PER_TILE
    tiles = jnp.arange(TILES, dtype=jnp.int32)
    active = (tile_a[:, None] <= tiles) & (tiles < tile_b[:, None])
    active = active.reshape(2, SOURCES, TILES).astype(jnp.int32)
    n = jnp.arange(SOURCES, dtype=jnp.int32)
    before = (n[None, :] < n[:, None]).astype(jnp.int32)
    rank = jnp.sum(before[None, :, :, None] * active[:, None], axis=2)
    pairs = (jnp.sum(active, axis=1) + 1) // 2
    earlier = (tiles[None, :] < tiles[:, None]).astype(jnp.int32)
    offset = jnp.sum(earlier[None] * pairs[:, None, :], axis=2)
    at = jnp.arange(ITEMS, dtype=jnp.int32)
    where = jnp.where(active == 1, offset[:, None, :] * 2 + rank, -1)
    where = where.reshape(2, 1, SOURCES * TILES)
    owner = jnp.repeat(n, TILES)[None, None] - SOURCES

    def owners(half):
        hit = where == (at * 2 + half)[None, :, None]
        return SOURCES + jnp.sum(jnp.where(hit, owner, 0), axis=2)

    done = (offset + pairs)[:, None, :] <= at[None, :, None]
    tile = jnp.minimum(jnp.sum(done.astype(jnp.int32), axis=2), TILES - 1)
    listed = owners(0) * 256 + owners(1) * 16 + tile
    return jnp.concatenate(
        [span_order, count, ordered, starts, place, jnp.sum(pairs, axis=1), listed.reshape(-1)]
    )


def body(queries, key_rows, value_rows, visit_ids, span_order):
    info = table(visit_ids, span_order)
    packed = pack(queries, key_rows, value_rows)
    packed = lax.all_to_all(packed, "zhi", 0, 0, tiled=True)
    spread, near_q = fan(packed)
    own = lax.all_to_all(
        spread, "plane", 0, 0, axis_index_groups=PLANE, tiled=True
    )
    far_q = lax.ppermute(near_q, "zlo", SWAP)
    other = lax.ppermute(own, "plane", [(i, i ^ 8) for i in range(32)])
    k, v = order_part(info, own)

    far_out, k, v = far_part(info, far_q, other, k, v)
    sent = lax.ppermute(far_out, "zlo", SWAP)
    near_out, mass = near_part(info, near_q, k, v)
    out = merge(near_out, mass, sent)
    out = lax.all_to_all(out, "zhi", 0, 0, tiled=True)
    return jnp.transpose(out, (1, 0, 2)).reshape(PIECE, HEADS * HEAD_DIM)


def solution(mesh):
    fine = Mesh(mesh.devices.reshape(8, 2, 32), ("zhi", "zlo", "plane"))
    rows = P(("zhi", "zlo", "plane"), None)
    return jax.shard_map(
        body,
        mesh=fine,
        in_specs=(rows, rows, rows, P(), P()),
        out_specs=rows,
        check_vma=False,
    )
```

```python
import jax
import jax.numpy as jnp
from jax import lax
from jax.experimental import pallas as pl
from jax.experimental.pallas import tpu as pltpu
from jax.sharding import Mesh, PartitionSpec as P

HEADS = 32
KV_HEADS = 8
HEAD_DIM = 128
GROUP = HEADS // KV_HEADS
SPAN_ROWS = 192
PIECE = 24
PARTS = SPAN_ROWS // PIECE
VISITS = 4
SPANS = 64
HALF = SPANS // 2
KEYS = HALF * SPAN_ROWS
PER_TILE = 4
UNROLL = 3
TILE = PER_TILE * SPAN_ROWS
TILES = KEYS // TILE
SOURCES = 8
ROWS = GROUP * PIECE
SCALE_LOG2 = HEAD_DIM ** (-0.5) * 1.4426950408889634
NOTHING = -3e38

ORDER = 0
COUNT = 64
SORTED = COUNT + 65
START = SORTED + HALF
YLO = START + VISITS
CORE = YLO + 1
ZLO = YLO + 2
FIRST = YLO + 3
TOTAL = YLO + 4
LIST = TOTAL + 2
ITEMS = SOURCES // 2 * TILES + UNROLL


def take_keys(info, src, side, k_buf, v_buf):
    zlo = info[ZLO]
    pieces = [buf.reshape(HALF * PARTS, PIECE, HEAD_DIM) for buf in (k_buf, v_buf)]

    def step(i, carry):
        k, half = i // 2, i % 2
        span = info[ORDER + (k * 2 + zlo) * 4 + half * 2 + side]
        rank = info[COUNT + span]
        for part in range(PARTS):
            for which, buf in enumerate(pieces):
                buf[rank * PARTS + part] = src[half * PARTS + part, k, which]
        return carry

    lax.fori_loop(0, 2 * SOURCES, step, 0)


def attend_sources(info, side, q_ref, k_buf, v_buf, scratch, put):
    s_buf, q_buf, low_buf, pos_buf, best, top_buf, total, acc = scratch
    ylo, core, first = info[YLO], info[CORE], info[FIRST]
    inside = lax.broadcasted_iota(jnp.int32, (PIECE, HEAD_DIM), 0)
    lane = lax.broadcasted_iota(jnp.int32, (1, HEAD_DIM), 1)

    def start_of(pos):
        low = jnp.zeros_like(pos)
        for v in range(1, VISITS):
            low = jnp.where(info[START + v] <= pos, info[START + v], low)
        return low

    for n in range(SOURCES):
        span = info[ORDER + (n * 2 + side) * 4 + ylo * 2 + core]
        pos = span * SPAN_ROWS + first + inside
        pos_buf[n] = pos
        low_buf[n] = start_of(pos)
        q_buf[n] = (
            q_ref[n].astype(jnp.float32).reshape(ROWS, HEAD_DIM).astype(jnp.bfloat16)
        )
        best[n] = jnp.full((ROWS, HEAD_DIM), -jnp.inf, jnp.float32)
        total[n] = jnp.zeros((ROWS, HEAD_DIM), jnp.float32)
        acc[n] = jnp.zeros((ROWS, HEAD_DIM), jnp.float32)
    far = jnp.where(side == info[ZLO], 0, 1)
    steps = (info[TOTAL + far] + UNROLL - 1) // UNROLL
    listed = LIST + far * ITEMS

    def item(at):
        entry = info[listed + at]
        return (entry // 256, entry // 16 % 16), entry % 16

    def scores(i, carry):
        for u in range(UNROLL):
            at = i * UNROLL + u
            slots, j = item(at)
            sources = [jnp.minimum(slot, SOURCES - 1) for slot in slots]
            both = lax.dot_general(
                jnp.concatenate([q_buf[n] for n in sources], axis=0),
                k_buf[pl.ds(pl.multiple_of(j * TILE, TILE), TILE), :],
                (((1,), (1,)), ((), ())),
                preferred_element_type=jnp.float32,
            )
            base = [
                (info[SORTED + j * PER_TILE + w] - w) * SPAN_ROWS for w in range(PER_TILE)
            ]
            keys = []
            for c in range(TILE // HEAD_DIM):
                left = c * HEAD_DIM // SPAN_ROWS
                right = (c * HEAD_DIM + HEAD_DIM - 1) // SPAN_ROWS
                key = lane + c * HEAD_DIM
                if left == right:
                    key = key + base[left]
                else:
                    key = key + jnp.where(key < right * SPAN_ROWS, base[left], base[right])
                keys.append(key)
            for e in range(2):
                s = both[e * ROWS : (e + 1) * ROWS].reshape(GROUP, PIECE, TILE)
                low, pos = low_buf[sources[e]], pos_buf[sources[e]]
                high = best[slots[e]].reshape(GROUP, PIECE, HEAD_DIM)
                for c, key in enumerate(keys):
                    keep = (key >= low) & (key <= pos)
                    part = jnp.where(
                        keep[None], s[:, :, c * HEAD_DIM : (c + 1) * HEAD_DIM], -jnp.inf
                    )
                    s_buf[
                        at,
                        e * ROWS : (e + 1) * ROWS,
                        c * HEAD_DIM : (c + 1) * HEAD_DIM,
                    ] = part.reshape(ROWS, HEAD_DIM)
                    high = jnp.maximum(high, part)
                best[slots[e]] = high.reshape(ROWS, HEAD_DIM)
        return carry

    lax.fori_loop(0, steps, scores, 0)

    for n in range(SOURCES):
        top = jnp.max(best[n], axis=1, keepdims=True)
        top_buf[n] = jnp.broadcast_to(top, (ROWS, HEAD_DIM))

    def mix(i, carry):
        for u in range(UNROLL):
            at = i * UNROLL + u
            slots, j = item(at)
            rows = []
            for e in range(2):
                top = top_buf[jnp.minimum(slots[e], SOURCES - 1)]
                top = jnp.where(top > -jnp.inf, top, 0.0)
                part_sum = total[slots[e]]
                parts = []
                for c in range(TILE // HEAD_DIM):
                    part = s_buf[
                        at,
                        e * ROWS : (e + 1) * ROWS,
                        c * HEAD_DIM : (c + 1) * HEAD_DIM,
                    ]
                    w = jnp.exp2((part - top) * SCALE_LOG2)
                    part_sum = part_sum + w
                    parts.append(w.astype(jnp.bfloat16))
                total[slots[e]] = part_sum
                rows.append(jnp.concatenate(parts, axis=1))
            mixed = jnp.dot(
                jnp.concatenate(rows, axis=0),
                v_buf[pl.ds(pl.multiple_of(j * TILE, TILE), TILE), :],
                preferred_element_type=jnp.float32,
            )
            for e in range(2):
                acc[slots[e]] = acc[slots[e]] + mixed[e * ROWS : (e + 1) * ROWS]
        return carry

    lax.fori_loop(0, steps, mix, 0)

    for n in range(SOURCES):
        top = top_buf[n]
        whole, out = jnp.sum(total[n], axis=1, keepdims=True), acc[n]
        some = top > -jnp.inf
        safe = jnp.where(some, whole, 1.0)
        mass = jnp.where(some, top * SCALE_LOG2 + jnp.log2(safe), NOTHING)
        put(
            n,
            (out / safe).reshape(GROUP, PIECE, HEAD_DIM),
            mass.reshape(GROUP, PIECE, HEAD_DIM),
        )


def order_kernel(info, own_ref, k_buf, v_buf):
    take_keys(info, own_ref, info[CORE], k_buf, v_buf)


def far_kernel(info, q_ref, other_ref, k_half, v_half, o_ref, k_buf, v_buf, *scratch):
    take_keys(info, other_ref, 1 - info[CORE], k_buf, v_buf)
    lane = lax.broadcasted_iota(jnp.int32, (PIECE, HEAD_DIM), 1)

    packed = [jnp.zeros((PIECE, HEAD_DIM), jnp.float32)]

    def put(n, out, mass):
        o_ref[n * GROUP : (n + 1) * GROUP] = out.astype(jnp.bfloat16)
        high = mass.astype(jnp.bfloat16).astype(jnp.float32)
        rest = mass - high
        middle = rest.astype(jnp.bfloat16).astype(jnp.float32)
        for i, piece in enumerate((high, middle, rest - middle)):
            for g in range(GROUP):
                packed[0] = jnp.where(
                    lane == (n * GROUP + g) * 3 + i, piece[g], packed[0]
                )

    attend_sources(info, 1 - info[ZLO], q_ref, k_buf, v_buf, scratch, put)
    o_ref[SOURCES * GROUP] = packed[0].astype(jnp.bfloat16)


def near_kernel(info, q_ref, k_buf, v_buf, o_ref, m_ref, *scratch):
    def put(n, out, mass):
        o_ref[n] = out
        m_ref[n] = mass

    attend_sources(info, info[ZLO], q_ref, k_buf, v_buf, scratch, put)


def merge_kernel(near_ref, mass_ref, far_ref, o_ref):
    packed = far_ref[SOURCES * GROUP].astype(jnp.float32)
    for n in range(SOURCES):
        for g in range(GROUP):
            c = (n * GROUP + g) * 3
            a = mass_ref[n, g]
            b = (
                packed[:, c : c + 1] + packed[:, c + 1 : c + 2] + packed[:, c + 2 : c + 3]
            )
            m = jnp.maximum(a, b)
            wa, wb = jnp.exp2(a - m), jnp.exp2(b - m)
            out = (wa * near_ref[n, g] + wb * far_ref[n * GROUP + g].astype(jnp.float32)) / (wa + wb)
            o_ref[n, :, g * HEAD_DIM : (g + 1) * HEAD_DIM] = out.astype(jnp.bfloat16)


def pack_kernel(q_ref, k_ref, v_ref, o_ref):
    for h in range(KV_HEADS):
        o_ref[h, 0] = k_ref[:, h * HEAD_DIM : (h + 1) * HEAD_DIM]
        o_ref[h, 1] = v_ref[:, h * HEAD_DIM : (h + 1) * HEAD_DIM]
        for g in range(GROUP):
            c = (h * GROUP + g) * HEAD_DIM
            o_ref[h, 2 + g] = q_ref[:, c : c + HEAD_DIM]


def fan_kernel(packed_ref, o_ref, q_ref, sems):
    copies = [
        pltpu.make_async_copy(packed_ref.at[:, :2], o_ref.at[i], sems.at[i]) for i in range(16)
    ]
    for c in copies:
        c.start()
    q_ref[...] = packed_ref[:, 2:]
    for c in copies:
        c.wait()


SMEM = pl.BlockSpec(memory_space=pltpu.SMEM)
VMEM = pl.BlockSpec(memory_space=pltpu.VMEM)
ANY = pl.BlockSpec(memory_space=pl.ANY)
COST = pl.CostEstimate(flops=6_000_000_000, bytes_accessed=4_000_000, transcendentals=4_000_000)


def shape(*sizes, kind=jnp.bfloat16):
    return jax.ShapeDtypeStruct(sizes, kind)


SCRATCH = [
    pltpu.VMEM((ITEMS, 2 * ROWS, TILE), jnp.float32),
    pltpu.VMEM((SOURCES, ROWS, HEAD_DIM), jnp.bfloat16),
    pltpu.VMEM((SOURCES, PIECE, HEAD_DIM), jnp.int32),
    pltpu.VMEM((SOURCES, PIECE, HEAD_DIM), jnp.int32),
    pltpu.VMEM((SOURCES + 1, ROWS, HEAD_DIM), jnp.float32),
    pltpu.VMEM((SOURCES, ROWS, HEAD_DIM), jnp.float32),
    pltpu.VMEM((SOURCES + 1, ROWS, HEAD_DIM), jnp.float32),
    pltpu.VMEM((SOURCES + 1, ROWS, HEAD_DIM), jnp.float32),
]
SMALL = pltpu.CompilerParams(vmem_limit_bytes=8 << 20)
LIMIT = pltpu.CompilerParams(vmem_limit_bytes=40 << 20)


def order_part(info, own):
    return pl.pallas_call(
        order_kernel,
        out_shape=(shape(KEYS, HEAD_DIM), shape(KEYS, HEAD_DIM)),
        in_specs=[SMEM, VMEM],
        out_specs=(VMEM, VMEM),
        compiler_params=SMALL,
        cost_estimate=pl.CostEstimate(flops=0, bytes_accessed=6_000_000, transcendentals=0),
        name="order",
    )(info, own)


def far_part(info, q, other, k, v):
    return pl.pallas_call(
        far_kernel,
        out_shape=(
            shape(SOURCES * GROUP + 1, PIECE, HEAD_DIM),
            shape(KEYS, HEAD_DIM),
            shape(KEYS, HEAD_DIM),
        ),
        in_specs=[SMEM, VMEM, VMEM, VMEM, VMEM],
        out_specs=(VMEM, VMEM, VMEM),
        scratch_shapes=SCRATCH,
        input_output_aliases={3: 1, 4: 2},
        compiler_params=LIMIT,
        cost_estimate=COST,
        name="far",
    )(info, q, other, k, v)


def near_part(info, q, k, v):
    return pl.pallas_call(
        near_kernel,
        out_shape=(
            shape(SOURCES, GROUP, PIECE, HEAD_DIM, kind=jnp.float32),
            shape(SOURCES, GROUP, PIECE, HEAD_DIM, kind=jnp.float32),
        ),
        in_specs=[SMEM, VMEM, VMEM, VMEM],
        out_specs=(VMEM, VMEM),
        scratch_shapes=SCRATCH,
        compiler_params=LIMIT,
        cost_estimate=COST,
        name="near",
    )(info, q, k, v)


def merge(near, mass, far):
    return pl.pallas_call(
        merge_kernel,
        out_shape=shape(SOURCES, PIECE, GROUP * HEAD_DIM),
        in_specs=[VMEM, VMEM, VMEM],
        out_specs=VMEM,
        compiler_params=SMALL,
        name="merge",
    )(near, mass, far)


def pack(q, k, v):
    return pl.pallas_call(
        pack_kernel,
        out_shape=shape(KV_HEADS, GROUP + 2, PIECE, HEAD_DIM),
        in_specs=[VMEM, VMEM, VMEM],
        out_specs=VMEM,
        name="pack",
    )(q, k, v)


def fan(packed):
    return pl.pallas_call(
        fan_kernel,
        out_shape=(
            shape(16, SOURCES, 2, PIECE, HEAD_DIM),
            shape(SOURCES, GROUP, PIECE, HEAD_DIM),
        ),
        in_specs=[VMEM],
        out_specs=(ANY, VMEM),
        scratch_shapes=[pltpu.SemaphoreType.DMA((16,))],
        compiler_params=SMALL,
        name="fan",
    )(packed)


SWAP = [(0, 1), (1, 0)]
PLANE = [
    [((ylo * 2 + core) * 2 + yhi) * 4 + x for ylo in range(2) for yhi in range(2) for x in range(4)]
    for core in range(2)
]


def look(values, at):
    index = jnp.arange(values.shape[0], dtype=jnp.int32)
    return jnp.sum(jnp.where(at[:, None] == index[None, :], values[None, :], 0), axis=1)


def basics(visit_ids, span_order):
    zlo = lax.axis_index("zlo").astype(jnp.int32)
    block = jnp.arange(SPANS, dtype=jnp.int32)
    mine = (block // 4) % 2 == zlo
    upto = jnp.arange(SPANS + 1, dtype=jnp.int32)
    count = jnp.sum(
        (mine[None, :] & (span_order[None, :] < upto[:, None])).astype(jnp.int32), axis=1
    )
    ranks = jnp.arange(HALF, dtype=jnp.int32)
    ordered = jnp.sum((count[None, 1:] <= ranks[:, None]).astype(jnp.int32), axis=1)
    starts = jnp.sum(
        (visit_ids[None, :] < jnp.arange(VISITS, dtype=jnp.int32)[:, None]).astype(jnp.int32),
        axis=1,
    )
    return count, ordered, starts


def listing(span_order, count, ordered, starts):
    zlo = lax.axis_index("zlo").astype(jnp.int32)
    at = lax.axis_index("plane")
    place = jnp.stack([at // 16, at // 8 % 2, zlo, at % 8 * PIECE]).astype(jnp.int32)
    side = jnp.stack([zlo, 1 - zlo])[:, None]
    source = (jnp.arange(SOURCES, dtype=jnp.int32)[None] * 2 + side) * 4
    span = look(span_order, source.reshape(-1) + place[0] * 2 + place[1])
    p0 = span * SPAN_ROWS + place[3]
    low = jnp.max(jnp.where(starts[None, :] <= p0[:, None], starts[None, :], 0), axis=1)
    tile_a = look(count, low // SPAN_ROWS) // PER_TILE
    tile_b = (look(count, span + 1) + PER_TILE - 1) // PER_TILE
    tiles = jnp.arange(TILES, dtype=jnp.int32)
    active = (tile_a[:, None] <= tiles) & (tiles < tile_b[:, None])
    active = active.reshape(2, SOURCES, TILES).astype(jnp.int32)
    n = jnp.arange(SOURCES, dtype=jnp.int32)
    before = (n[None, :] < n[:, None]).astype(jnp.int32)
    rank = jnp.sum(before[None, :, :, None] * active[:, None], axis=2)
    pairs = (jnp.sum(active, axis=1) + 1) // 2
    earlier = (tiles[None, :] < tiles[:, None]).astype(jnp.int32)
    offset = jnp.sum(earlier[None] * pairs[:, None, :], axis=2)
    at = jnp.arange(ITEMS, dtype=jnp.int32)
    where = jnp.where(active == 1, offset[:, None, :] * 2 + rank, -1)
    where = where.reshape(2, 1, SOURCES * TILES)
    owner = jnp.repeat(n, TILES)[None, None] - SOURCES

    def owners(half):
        hit = where == (at * 2 + half)[None, :, None]
        return SOURCES + jnp.sum(jnp.where(hit, owner, 0), axis=2)

    done = (offset + pairs)[:, None, :] <= at[None, :, None]
    tile = jnp.minimum(jnp.sum(done.astype(jnp.int32), axis=2), TILES - 1)
    listed = owners(0) * 256 + owners(1) * 16 + tile
    return jnp.concatenate(
        [span_order, count, ordered, starts, place, jnp.sum(pairs, axis=1), listed.reshape(-1)]
    )


def body(queries, key_rows, value_rows, visit_ids, span_order):
    basic = basics(visit_ids, span_order)
    packed = pack(queries, key_rows, value_rows)
    packed = lax.all_to_all(packed, "zhi", 0, 0, tiled=True)
    spread, near_q = fan(packed)
    info = listing(span_order, *basic)
    own = lax.all_to_all(
        spread, "plane", 0, 0, axis_index_groups=PLANE, tiled=True
    )
    far_q = lax.ppermute(near_q, "zlo", SWAP)
    other = lax.ppermute(own, "plane", [(i, i ^ 8) for i in range(32)])
    k, v = order_part(info, own)

    far_out, k, v = far_part(info, far_q, other, k, v)
    sent = lax.ppermute(far_out, "zlo", SWAP)
    near_out, mass = near_part(info, near_q, k, v)
    out = merge(near_out, mass, sent)
    out = lax.all_to_all(out, "zhi", 0, 0, tiled=True)
    return jnp.transpose(out, (1, 0, 2)).reshape(PIECE, HEADS * HEAD_DIM)


def solution(mesh):
    fine = Mesh(mesh.devices.reshape(8, 2, 32), ("zhi", "zlo", "plane"))
    rows = P(("zhi", "zlo", "plane"), None)
    return jax.shard_map(
        body,
        mesh=fine,
        in_specs=(rows, rows, rows, P(), P()),
        out_specs=rows,
        check_vma=False,
    )
```

```python
import jax
import jax.numpy as jnp
from jax import lax
from jax.experimental import pallas as pl
from jax.experimental.pallas import tpu as pltpu
from jax.sharding import Mesh, PartitionSpec as P

HEADS = 32
KV_HEADS = 8
HEAD_DIM = 128
GROUP = HEADS // KV_HEADS
SPAN_ROWS = 192
PIECE = 24
PARTS = SPAN_ROWS // PIECE
VISITS = 4
SPANS = 64
HALF = SPANS // 2
KEYS = HALF * SPAN_ROWS
PER_TILE = 4
UNROLL = 3
DEPTH = 256
TILE = PER_TILE * SPAN_ROWS
TILES = KEYS // TILE
SOURCES = 8
ROWS = GROUP * PIECE
SCALE_LOG2 = HEAD_DIM ** (-0.5) * 1.4426950408889634
NOTHING = -3e38

ORDER = 0
COUNT = 64
SORTED = COUNT + 65
START = SORTED + HALF
YLO = START + VISITS
CORE = YLO + 1
ZLO = YLO + 2
FIRST = YLO + 3
TOTAL = YLO + 4
LIST = TOTAL + 2
ITEMS = SOURCES // 2 * TILES + UNROLL


def take_keys(info, src, side, k_buf, v_buf):
    zlo = info[ZLO]
    pieces = [buf.reshape(HALF * PARTS, PIECE, HEAD_DIM) for buf in (k_buf, v_buf)]

    def step(i, carry):
        k, half = i // 2, i % 2
        span = info[ORDER + (k * 2 + zlo) * 4 + half * 2 + side]
        rank = info[COUNT + span]
        for part in range(PARTS):
            for which, buf in enumerate(pieces):
                buf[rank * PARTS + part] = src[half * PARTS + part, k, which]
        return carry

    lax.fori_loop(0, 2 * SOURCES, step, 0)


def attend_sources(info, side, q_ref, k_buf, v_buf, scratch, put):
    s_buf, q_buf, low_buf, pos_buf, best, top_buf, total, acc = scratch
    ylo, core, first = info[YLO], info[CORE], info[FIRST]
    inside = lax.broadcasted_iota(jnp.int32, (PIECE, HEAD_DIM), 0)
    lane = lax.broadcasted_iota(jnp.int32, (1, HEAD_DIM), 1)

    def start_of(pos):
        low = jnp.zeros_like(pos)
        for v in range(1, VISITS):
            low = jnp.where(info[START + v] <= pos, info[START + v], low)
        return low

    for n in range(SOURCES):
        span = info[ORDER + (n * 2 + side) * 4 + ylo * 2 + core]
        pos = span * SPAN_ROWS + first + inside
        pos_buf[n] = pos
        low_buf[n] = start_of(pos)
        q_buf[n] = (
            q_ref[n].astype(jnp.float32).reshape(ROWS, HEAD_DIM).astype(jnp.bfloat16)
        )
        best[n] = jnp.full((ROWS, HEAD_DIM), -jnp.inf, jnp.float32)
        total[n] = jnp.zeros((ROWS, HEAD_DIM), jnp.float32)
        acc[n] = jnp.zeros((ROWS, HEAD_DIM), jnp.float32)
    far = jnp.where(side == info[ZLO], 0, 1)
    steps = (info[TOTAL + far] + UNROLL - 1) // UNROLL
    listed = LIST + far * ITEMS

    def item(at):
        entry = info[listed + at]
        return (entry // 256, entry // 16 % 16), entry % 16

    def scores(i, carry):
        for u in range(UNROLL):
            at = i * UNROLL + u
            slots, j = item(at)
            sources = [jnp.minimum(slot, SOURCES - 1) for slot in slots]
            both = lax.dot_general(
                jnp.concatenate([q_buf[n] for n in sources], axis=0),
                k_buf[pl.ds(pl.multiple_of(j * TILE, TILE), TILE), :],
                (((1,), (1,)), ((), ())),
                preferred_element_type=jnp.float32,
            )
            base = [
                (info[SORTED + j * PER_TILE + w] - w) * SPAN_ROWS for w in range(PER_TILE)
            ]
            keys = []
            for c in range(TILE // HEAD_DIM):
                left = c * HEAD_DIM // SPAN_ROWS
                right = (c * HEAD_DIM + HEAD_DIM - 1) // SPAN_ROWS
                key = lane + c * HEAD_DIM
                if left == right:
                    key = key + base[left]
                else:
                    key = key + jnp.where(key < right * SPAN_ROWS, base[left], base[right])
                keys.append(key)
            for e in range(2):
                s = both[e * ROWS : (e + 1) * ROWS].reshape(GROUP, PIECE, TILE)
                low, pos = low_buf[sources[e]], pos_buf[sources[e]]
                high = best[slots[e]].reshape(GROUP, PIECE, HEAD_DIM)
                for c, key in enumerate(keys):
                    keep = (key >= low) & (key <= pos)
                    part = jnp.where(
                        keep[None], s[:, :, c * HEAD_DIM : (c + 1) * HEAD_DIM], -jnp.inf
                    )
                    s_buf[
                        at,
                        e * ROWS : (e + 1) * ROWS,
                        c * HEAD_DIM : (c + 1) * HEAD_DIM,
                    ] = part.reshape(ROWS, HEAD_DIM)
                    high = jnp.maximum(high, part)
                best[slots[e]] = high.reshape(ROWS, HEAD_DIM)
        return carry

    lax.fori_loop(0, steps, scores, 0)

    for n in range(SOURCES):
        top = jnp.max(best[n], axis=1, keepdims=True)
        top_buf[n] = jnp.broadcast_to(top, (ROWS, HEAD_DIM))

    def mix(i, carry):
        for u in range(UNROLL):
            at = i * UNROLL + u
            slots, j = item(at)
            tops = []
            for slot in slots:
                top = top_buf[jnp.minimum(slot, SOURCES - 1)]
                tops.append(jnp.where(top > -jnp.inf, top, 0.0))
            sums = [total[slot] for slot in slots]
            mixed = jnp.zeros((2 * ROWS, HEAD_DIM), jnp.float32)
            for d in range(0, TILE, DEPTH):
                rows = []
                for e in range(2):
                    parts = []
                    for c in range(d, d + DEPTH, HEAD_DIM):
                        part = s_buf[at, e * ROWS : (e + 1) * ROWS, c : c + HEAD_DIM]
                        w = jnp.exp2((part - tops[e]) * SCALE_LOG2)
                        sums[e] = sums[e] + w
                        parts.append(w.astype(jnp.bfloat16))
                    rows.append(jnp.concatenate(parts, axis=1))
                mixed = mixed + jnp.dot(
                    jnp.concatenate(rows, axis=0),
                    v_buf[pl.ds(pl.multiple_of(j * TILE + d, DEPTH), DEPTH), :],
                    preferred_element_type=jnp.float32,
                )
            for e in range(2):
                total[slots[e]] = sums[e]
            for e in range(2):
                acc[slots[e]] = acc[slots[e]] + mixed[e * ROWS : (e + 1) * ROWS]
        return carry

    lax.fori_loop(0, steps, mix, 0)

    for n in range(SOURCES):
        top = top_buf[n]
        whole, out = jnp.sum(total[n], axis=1, keepdims=True), acc[n]
        some = top > -jnp.inf
        safe = jnp.where(some, whole, 1.0)
        mass = jnp.where(some, top * SCALE_LOG2 + jnp.log2(safe), NOTHING)
        put(
            n,
            (out / safe).reshape(GROUP, PIECE, HEAD_DIM),
            mass.reshape(GROUP, PIECE, HEAD_DIM),
        )


def order_kernel(info, own_ref, k_buf, v_buf):
    take_keys(info, own_ref, info[CORE], k_buf, v_buf)


def far_kernel(info, q_ref, other_ref, k_half, v_half, o_ref, k_buf, v_buf, *scratch):
    take_keys(info, other_ref, 1 - info[CORE], k_buf, v_buf)
    lane = lax.broadcasted_iota(jnp.int32, (PIECE, HEAD_DIM), 1)

    packed = [jnp.zeros((PIECE, HEAD_DIM), jnp.float32)]

    def put(n, out, mass):
        o_ref[n * GROUP : (n + 1) * GROUP] = out.astype(jnp.bfloat16)
        high = mass.astype(jnp.bfloat16).astype(jnp.float32)
        rest = mass - high
        middle = rest.astype(jnp.bfloat16).astype(jnp.float32)
        for i, piece in enumerate((high, middle, rest - middle)):
            for g in range(GROUP):
                packed[0] = jnp.where(
                    lane == (n * GROUP + g) * 3 + i, piece[g], packed[0]
                )

    attend_sources(info, 1 - info[ZLO], q_ref, k_buf, v_buf, scratch, put)
    o_ref[SOURCES * GROUP] = packed[0].astype(jnp.bfloat16)


def near_kernel(info, q_ref, k_buf, v_buf, o_ref, m_ref, *scratch):
    def put(n, out, mass):
        o_ref[n] = out
        m_ref[n] = mass

    attend_sources(info, info[ZLO], q_ref, k_buf, v_buf, scratch, put)


def merge_kernel(near_ref, mass_ref, far_ref, o_ref):
    packed = far_ref[SOURCES * GROUP].astype(jnp.float32)
    for n in range(SOURCES):
        for g in range(GROUP):
            c = (n * GROUP + g) * 3
            a = mass_ref[n, g]
            b = (
                packed[:, c : c + 1] + packed[:, c + 1 : c + 2] + packed[:, c + 2 : c + 3]
            )
            m = jnp.maximum(a, b)
            wa, wb = jnp.exp2(a - m), jnp.exp2(b - m)
            out = (wa * near_ref[n, g] + wb * far_ref[n * GROUP + g].astype(jnp.float32)) / (wa + wb)
            o_ref[n, :, g * HEAD_DIM : (g + 1) * HEAD_DIM] = out.astype(jnp.bfloat16)


def pack_kernel(q_ref, k_ref, v_ref, o_ref):
    for h in range(KV_HEADS):
        o_ref[h, 0] = k_ref[:, h * HEAD_DIM : (h + 1) * HEAD_DIM]
        o_ref[h, 1] = v_ref[:, h * HEAD_DIM : (h + 1) * HEAD_DIM]
        for g in range(GROUP):
            c = (h * GROUP + g) * HEAD_DIM
            o_ref[h, 2 + g] = q_ref[:, c : c + HEAD_DIM]


def fan_kernel(packed_ref, o_ref, q_ref, sems):
    copies = [
        pltpu.make_async_copy(packed_ref.at[:, :2], o_ref.at[i], sems.at[i]) for i in range(16)
    ]
    for c in copies:
        c.start()
    q_ref[...] = packed_ref[:, 2:]
    for c in copies:
        c.wait()


SMEM = pl.BlockSpec(memory_space=pltpu.SMEM)
VMEM = pl.BlockSpec(memory_space=pltpu.VMEM)
ANY = pl.BlockSpec(memory_space=pl.ANY)
COST = pl.CostEstimate(flops=6_000_000_000, bytes_accessed=4_000_000, transcendentals=4_000_000)


def shape(*sizes, kind=jnp.bfloat16):
    return jax.ShapeDtypeStruct(sizes, kind)


SCRATCH = [
    pltpu.VMEM((ITEMS, 2 * ROWS, TILE), jnp.float32),
    pltpu.VMEM((SOURCES, ROWS, HEAD_DIM), jnp.bfloat16),
    pltpu.VMEM((SOURCES, PIECE, HEAD_DIM), jnp.int32),
    pltpu.VMEM((SOURCES, PIECE, HEAD_DIM), jnp.int32),
    pltpu.VMEM((SOURCES + 1, ROWS, HEAD_DIM), jnp.float32),
    pltpu.VMEM((SOURCES, ROWS, HEAD_DIM), jnp.float32),
    pltpu.VMEM((SOURCES + 1, ROWS, HEAD_DIM), jnp.float32),
    pltpu.VMEM((SOURCES + 1, ROWS, HEAD_DIM), jnp.float32),
]
SMALL = pltpu.CompilerParams(vmem_limit_bytes=8 << 20)
LIMIT = pltpu.CompilerParams(vmem_limit_bytes=40 << 20)


def order_part(info, own):
    return pl.pallas_call(
        order_kernel,
        out_shape=(shape(KEYS, HEAD_DIM), shape(KEYS, HEAD_DIM)),
        in_specs=[SMEM, VMEM],
        out_specs=(VMEM, VMEM),
        compiler_params=SMALL,
        cost_estimate=pl.CostEstimate(flops=0, bytes_accessed=6_000_000, transcendentals=0),
        name="order",
    )(info, own)


def far_part(info, q, other, k, v):
    return pl.pallas_call(
        far_kernel,
        out_shape=(
            shape(SOURCES * GROUP + 1, PIECE, HEAD_DIM),
            shape(KEYS, HEAD_DIM),
            shape(KEYS, HEAD_DIM),
        ),
        in_specs=[SMEM, VMEM, VMEM, VMEM, VMEM],
        out_specs=(VMEM, VMEM, VMEM),
        scratch_shapes=SCRATCH,
        input_output_aliases={3: 1, 4: 2},
        compiler_params=LIMIT,
        cost_estimate=COST,
        name="far",
    )(info, q, other, k, v)


def near_part(info, q, k, v):
    return pl.pallas_call(
        near_kernel,
        out_shape=(
            shape(SOURCES, GROUP, PIECE, HEAD_DIM, kind=jnp.float32),
            shape(SOURCES, GROUP, PIECE, HEAD_DIM, kind=jnp.float32),
        ),
        in_specs=[SMEM, VMEM, VMEM, VMEM],
        out_specs=(VMEM, VMEM),
        scratch_shapes=SCRATCH,
        compiler_params=LIMIT,
        cost_estimate=COST,
        name="near",
    )(info, q, k, v)


def merge(near, mass, far):
    return pl.pallas_call(
        merge_kernel,
        out_shape=shape(SOURCES, PIECE, GROUP * HEAD_DIM),
        in_specs=[VMEM, VMEM, VMEM],
        out_specs=VMEM,
        compiler_params=SMALL,
        name="merge",
    )(near, mass, far)


def pack(q, k, v):
    return pl.pallas_call(
        pack_kernel,
        out_shape=shape(KV_HEADS, GROUP + 2, PIECE, HEAD_DIM),
        in_specs=[VMEM, VMEM, VMEM],
        out_specs=VMEM,
        name="pack",
    )(q, k, v)


def fan(packed):
    return pl.pallas_call(
        fan_kernel,
        out_shape=(
            shape(16, SOURCES, 2, PIECE, HEAD_DIM),
            shape(SOURCES, GROUP, PIECE, HEAD_DIM),
        ),
        in_specs=[VMEM],
        out_specs=(ANY, VMEM),
        scratch_shapes=[pltpu.SemaphoreType.DMA((16,))],
        compiler_params=SMALL,
        name="fan",
    )(packed)


SWAP = [(0, 1), (1, 0)]
PLANE = [
    [((ylo * 2 + core) * 2 + yhi) * 4 + x for ylo in range(2) for yhi in range(2) for x in range(4)]
    for core in range(2)
]


def look(values, at):
    index = jnp.arange(values.shape[0], dtype=jnp.int32)
    return jnp.sum(jnp.where(at[:, None] == index[None, :], values[None, :], 0), axis=1)


def basics(visit_ids, span_order):
    zlo = lax.axis_index("zlo").astype(jnp.int32)
    block = jnp.arange(SPANS, dtype=jnp.int32)
    mine = (block // 4) % 2 == zlo
    upto = jnp.arange(SPANS + 1, dtype=jnp.int32)
    count = jnp.sum(
        (mine[None, :] & (span_order[None, :] < upto[:, None])).astype(jnp.int32), axis=1
    )
    ranks = jnp.arange(HALF, dtype=jnp.int32)
    ordered = jnp.sum((count[None, 1:] <= ranks[:, None]).astype(jnp.int32), axis=1)
    starts = jnp.sum(
        (visit_ids[None, :] < jnp.arange(VISITS, dtype=jnp.int32)[:, None]).astype(jnp.int32),
        axis=1,
    )
    return count, ordered, starts


def listing(span_order, count, ordered, starts):
    zlo = lax.axis_index("zlo").astype(jnp.int32)
    at = lax.axis_index("plane")
    place = jnp.stack([at // 16, at // 8 % 2, zlo, at % 8 * PIECE]).astype(jnp.int32)
    side = jnp.stack([zlo, 1 - zlo])[:, None]
    source = (jnp.arange(SOURCES, dtype=jnp.int32)[None] * 2 + side) * 4
    span = look(span_order, source.reshape(-1) + place[0] * 2 + place[1])
    p0 = span * SPAN_ROWS + place[3]
    low = jnp.max(jnp.where(starts[None, :] <= p0[:, None], starts[None, :], 0), axis=1)
    tile_a = look(count, low // SPAN_ROWS) // PER_TILE
    tile_b = (look(count, span + 1) + PER_TILE - 1) // PER_TILE
    tiles = jnp.arange(TILES, dtype=jnp.int32)
    active = (tile_a[:, None] <= tiles) & (tiles < tile_b[:, None])
    active = active.reshape(2, SOURCES, TILES).astype(jnp.int32)
    n = jnp.arange(SOURCES, dtype=jnp.int32)
    before = (n[None, :] < n[:, None]).astype(jnp.int32)
    rank = jnp.sum(before[None, :, :, None] * active[:, None], axis=2)
    pairs = (jnp.sum(active, axis=1) + 1) // 2
    earlier = (tiles[None, :] < tiles[:, None]).astype(jnp.int32)
    offset = jnp.sum(earlier[None] * pairs[:, None, :], axis=2)
    at = jnp.arange(ITEMS, dtype=jnp.int32)
    where = jnp.where(active == 1, offset[:, None, :] * 2 + rank, -1)
    where = where.reshape(2, 1, SOURCES * TILES)
    owner = jnp.repeat(n, TILES)[None, None] - SOURCES

    def owners(half):
        hit = where == (at * 2 + half)[None, :, None]
        return SOURCES + jnp.sum(jnp.where(hit, owner, 0), axis=2)

    done = (offset + pairs)[:, None, :] <= at[None, :, None]
    tile = jnp.minimum(jnp.sum(done.astype(jnp.int32), axis=2), TILES - 1)
    listed = owners(0) * 256 + owners(1) * 16 + tile
    return jnp.concatenate(
        [span_order, count, ordered, starts, place, jnp.sum(pairs, axis=1), listed.reshape(-1)]
    )


def body(queries, key_rows, value_rows, visit_ids, span_order):
    basic = basics(visit_ids, span_order)
    packed = pack(queries, key_rows, value_rows)
    packed = lax.all_to_all(packed, "zhi", 0, 0, tiled=True)
    spread, near_q = fan(packed)
    info = listing(span_order, *basic)
    own = lax.all_to_all(
        spread, "plane", 0, 0, axis_index_groups=PLANE, tiled=True
    )
    far_q = lax.ppermute(near_q, "zlo", SWAP)
    other = lax.ppermute(own, "plane", [(i, i ^ 8) for i in range(32)])
    k, v = order_part(info, own)

    far_out, k, v = far_part(info, far_q, other, k, v)
    sent = lax.ppermute(far_out, "zlo", SWAP)
    near_out, mass = near_part(info, near_q, k, v)
    out = merge(near_out, mass, sent)
    out = lax.all_to_all(out, "zhi", 0, 0, tiled=True)
    return jnp.transpose(out, (1, 0, 2)).reshape(PIECE, HEADS * HEAD_DIM)


def solution(mesh):
    fine = Mesh(mesh.devices.reshape(8, 2, 32), ("zhi", "zlo", "plane"))
    rows = P(("zhi", "zlo", "plane"), None)
    return jax.shard_map(
        body,
        mesh=fine,
        in_specs=(rows, rows, rows, P(), P()),
        out_specs=rows,
        check_vma=False,
    )
```
